32 devices in a mesh: tm: 2 (over x), slope: 4 (over y, core), act: 4 (over z).
Axes of the slice: x: 2, y: 2, z: 4, core: 2. Of those that a mesh axis runs over, the one named last changes fastest.
Arguments:
- frames: bfloat16 [16384, 1024], P('tm', 'slope'), may hold values from -6 to 6
- frame_scale: float32 [16384], P('tm'), may hold values from 0.5 to 2
- codes: int32 [16384], P('act'), may hold values from 0 to 16383, each once
- assign: int32 [1024], replicated, may hold values from 0 to 2
- loads: float32 [3], replicated, may hold values from 0.3 to 3
Outputs:
- gram_panel: float32 [16384, 1024], P('act')
- factor: float32 [1024, 1024], P('act')
The draws below stay inside these ranges and needn't reach their ends.
Inputs may be any that keep to these rules, and one draw needn't show every extreme that they name: `codes`: each actuator has its own Hadamard row.
All inputs are finite; a program needn't handle non-finite values.
Results may differ from the reference program's by a relative error of at most 0.0055.
Values may be sent and summed in bfloat16 or wider, within the bound.
No kernel may reach another device: no remote copies, remote signals or barrier semaphores. Data moves between devices by JAX's collectives and lax.ppermute only.
A program may use at most 128 MiB of HBM per device.

```python
import math
import jax
import jax.numpy as jnp
from jax import lax

NA = 16384
PW = 1024
NDM = 3
FRAMES = 16384
NS = 1024


def with_ends(entries, stream_key, low, top_value):
    spot = [jax.random.randint(jax.random.fold_in(stream_key, axis), (), 0, length) for axis, length in enumerate(entries.shape)]
    widest = entries.shape.index(max(entries.shape))
    next_to = spot[:widest] + [(spot[widest] + 1) % entries.shape[widest]] + spot[widest + 1:]
    return entries.at[tuple(spot)].set(low).at[tuple(next_to)].set(top_value)


def block_scale(own_key, extent, split, least, largest):
    def one(position, blocks):
        draws = jax.random.uniform(jax.random.fold_in(jax.random.fold_in(own_key, 6), position), (blocks,), jnp.float32, least / len(split), largest / len(split))
        return jnp.repeat(jnp.exp(draws), extent[position] // blocks).reshape((-1,) + (1,) * (len(extent) - position - 1))

    gain = one(*split[0])
    for cut in split[1:]:
        gain = gain * one(*cut)
    return gain


def gaussian(own_key, dims, width, bound, shards=(), kind=jnp.bfloat16):
    values = jax.random.normal(own_key, dims, jnp.float32) * width
    if len(shards) > 0:
        values = block_scale(own_key, dims, shards, -0.22, 0.18) * values
    return jnp.clip(values, min=-bound, max=bound).astype(kind)


def setup_inputs(seed: int = 0) -> dict:
    keys = jax.random.split(jax.random.key(seed), 6)
    return {
        "frames": gaussian(keys[0], (FRAMES, NS), 1.0, 6.0, ((0, 2), (1, 4))),
        "frame_scale": jnp.clip(jnp.exp(math.log(2.0) - 1.3862944 * jax.random.uniform(keys[1], (FRAMES,), jnp.float32) ** block_scale(keys[1], (FRAMES,), ((0, 2),), -0.2, 0.2)), 0.5, 2.0),
        "codes": jax.random.permutation(keys[2], NA).astype(jnp.int32),
        "assign": with_ends(jax.random.randint(keys[3], (PW,), 0, NDM), jax.random.fold_in(keys[3], 1), 0, NDM - 1).astype(jnp.int32),
        "loads": jnp.clip(jnp.exp(jax.random.uniform(keys[4], (NDM,), jnp.float32, math.log(0.3), math.log(3.0))), 0.3, 3.0),
    }


def parity_bits(values):
    folded = values
    for shift_by in (16, 8, 4, 2, 1):
        folded = jnp.bitwise_xor(folded, jnp.right_shift(folded, shift_by))
    return jnp.bitwise_and(folded, 1)

def reference(frames, frame_scale, codes, assign, loads):
    frames32 = frames.astype(jnp.float32)
    frame_ids = lax.broadcasted_iota(jnp.int32, (FRAMES, PW), 0)
    code_blocks = codes.reshape(NA // PW, PW)

    def demod_block(code_row):
        parity = parity_bits(jnp.bitwise_and(frame_ids, code_row[None, :]))
        weights = ((1 - 2 * parity).astype(jnp.float32) * frame_scale[:, None]).astype(jnp.bfloat16)
        return jnp.dot(frames32.T.astype(jnp.float32), weights.astype(jnp.float32), precision=lax.Precision.HIGHEST, preferred_element_type=jnp.float32)
    blocks = lax.map(demod_block, code_blocks)
    summed = jnp.transpose(blocks, (1, 0, 2)).reshape(NS, NA)
    im_matrix = (summed * (1.0 / FRAMES ** 0.5)).astype(jnp.bfloat16).astype(jnp.float32)
    gram_panel = jnp.dot(im_matrix.T.astype(jnp.float32), im_matrix[:, :PW].astype(jnp.float32), precision=lax.Precision.HIGHEST, preferred_element_type=jnp.float32) / float(NS)
    load_col = loads[assign]
    loaded = gram_panel[:PW] + jnp.diag(load_col)
    factor = jnp.linalg.cholesky(loaded)
    return (gram_panel, factor)
```

```python
import functools
import math

import jax
import jax.numpy as jnp
from jax import lax
from jax.experimental import pallas as pl
from jax.experimental.pallas import tpu as pltpu
from jax.sharding import PartitionSpec as P

PW = 1024
NDM = 3
F32 = jnp.float32
BF16 = jnp.bfloat16
LO = 256
B = 128
HIGHEST = lax.Precision.HIGHEST


def parity_bits(values):
    for shift_by in (16, 8, 4, 2, 1):
        values = jnp.bitwise_xor(values, jnp.right_shift(values, shift_by))
    return jnp.bitwise_and(values, 1)


def demod_kernel(codes, sgn, x_ref, w_ref, o_ref, had, tab, *, n_hi, n_top, group):
    i = pl.program_id(0)
    s = x_ref.shape[1]
    per = x_ref.shape[0] // LO

    @pl.when(i == 0)
    def _():
        r = lax.broadcasted_iota(jnp.int32, (LO, LO), 0)
        c = lax.broadcasted_iota(jnp.int32, (LO, LO), 1)
        had[...] = (1 - 2 * parity_bits(r & c)).astype(F32)

    for k in range(per):
        weights = (had[...] * w_ref[k : k + 1, :]).astype(BF16)
        tab[pl.ds(i * per + k, 1)] = jnp.dot(
            weights, x_ref[k * LO : (k + 1) * LO, :], preferred_element_type=F32
        )[None]

    @pl.when(i == pl.num_programs(0) - 1)
    def _():
        def column(t, _):
            rows = pl.ds(pl.multiple_of(t * 8, 8), 8)
            for l in range(s // 128):
                lanes = slice(l * 128, (l + 1) * 128)
                v = [tab[h, rows, lanes] for h in range(n_hi)]
                step = 1
                while step < n_hi:
                    for a in range(n_hi):
                        if not a & step:
                            v[a], v[a + step] = v[a] + v[a + step], v[a] - v[a + step]
                    step *= 2
                for h in range(n_hi):
                    tab[h, rows, lanes] = v[h]
                    for j in range(1, n_top):
                        tab[j * n_hi + h, rows, lanes] = v[h] * sgn[j]
            return 0

        lax.fori_loop(0, LO // 8, column, 0)
        flat = tab.reshape(n_top * n_hi * LO, s)

        def gather(t, _):
            base = pl.multiple_of(t * group, group)
            rows = [flat[pl.ds(codes[base + m], 1), :] for m in range(group)]
            o_ref[pl.ds(base, group), :] = jnp.concatenate(rows, axis=0).astype(BF16)
            return 0

        lax.fori_loop(0, o_ref.shape[0] // group, gather, 0)


def demod(frames, scale_rows, codes, sgn, per=8, group=16):
    f, s = frames.shape
    n = codes.shape[0]
    n_hi = f // LO
    n_top = sgn.shape[0]
    return pl.pallas_call(
        functools.partial(demod_kernel, n_hi=n_hi, n_top=n_top, group=group),
        out_shape=jax.ShapeDtypeStruct((n, s), BF16),
        grid_spec=pltpu.PrefetchScalarGridSpec(
            num_scalar_prefetch=2,
            grid=(n_hi // per,),
            in_specs=[
                pl.BlockSpec((per * LO, s), lambda i, *_: (i, 0)),
                pl.BlockSpec((per, LO), lambda i, *_: (i, 0)),
            ],
            out_specs=pl.BlockSpec((n, s), lambda i, *_: (0, 0)),
            scratch_shapes=[
                pltpu.VMEM((LO, LO), F32),
                pltpu.VMEM((n_top * n_hi, LO, s), F32),
            ],
        ),
        cost_estimate=pl.CostEstimate(
            flops=2 * f * LO * s, bytes_accessed=2 * f * s + 2 * n * s, transcendentals=0
        ),
        compiler_params=pltpu.CompilerParams(
            vmem_limit_bytes=40 << 20, dimension_semantics=("arbitrary",)
        ),
    )(codes, sgn, frames, scale_rows)


def across(v, lane):
    return jnp.broadcast_to(v[:, lane : lane + 1], (8, 128))


def down(v, row):
    return jnp.broadcast_to(v[row : row + 1, :], (8, 128))


def factor_tile(tile):
    lanes = lax.broadcasted_iota(jnp.int32, (8, 128), 1)
    subs = lax.broadcasted_iota(jnp.int32, (8, 128), 0)
    n = B // 8
    m = [tile[8 * g : 8 * g + 8, :] for g in range(n)]
    e = [jnp.where(lanes == subs + 8 * g, 1.0, 0.0).astype(F32) for g in range(n)]
    upper, inverse = [], []
    for q in range(n):
        cols = [across(m[q], 8 * q + j) for j in range(8)]
        s = {(i, j): down(cols[j], i) for j in range(8) for i in range(j, 8)}
        r = [down(m[q], i) for i in range(8)]
        t = [down(e[q], i) for i in range(8)]
        if q + 1 < n:
            c = [across(m[q + 1], 8 * q + j) for j in range(8)]
            m_next, e_next = m[q + 1], e[q + 1]
        far = {g: [across(m[g], 8 * q + j) for j in range(8)] for g in range(q + 2, n)}
        inv, u, w = [], [], []
        for j in range(8):
            root = lax.rsqrt(s[j, j])
            inv.append(root)
            l = {i: s[i, j] * root for i in range(j + 1, 8)}
            for i in range(j + 1, 8):
                for k in range(j + 1, i + 1):
                    s[i, k] = s[i, k] - l[i] * l[k]
                s[i, j] = l[i]
            u.append(r[j] * root)
            w.append(t[j] * root)
            for i in range(j + 1, 8):
                r[i] = r[i] - l[i] * u[j]
                t[i] = t[i] - l[i] * w[j]
            if q + 1 < n:
                lb = c[j] * root
                for k in range(j + 1, 8):
                    c[k] = c[k] - lb * l[k]
                m_next = m_next - lb * u[j]
                e_next = e_next - lb * w[j]
        u_rows, w_rows = u[0], w[0]
        for j in range(1, 8):
            u_rows = jnp.where(subs == j, u[j], u_rows)
            w_rows = jnp.where(subs == j, w[j], w_rows)
        upper.append(jnp.where(lanes >= subs + 8 * q, u_rows, 0.0))
        inverse.append(w_rows)
        if q + 1 < n:
            m[q + 1], e[q + 1] = m_next, e_next
        if q + 2 < n:
            ug, wg = [None] * 8, [None] * 8
            for j in reversed(range(8)):
                a, b = u[j], w[j]
                for i in range(j + 1, 8):
                    a = a - s[i, j] * ug[i]
                    b = b - s[i, j] * wg[i]
                ug[j], wg[j] = a * inv[j], b * inv[j]
            for g in range(q + 2, n):
                for j in range(8):
                    m[g] = m[g] - far[g][j] * ug[j]
                    e[g] = e[g] - far[g][j] * wg[j]
    return upper, inverse


def factor_kernel(pos, *refs, n_slope, total_rows, block):
    pieces = refs[:n_slope]
    load_ref, o_ref, panel, u_ref, inverse, rows = refs[n_slope:]
    width = pieces[0].shape[0]
    s_dev = pieces[0].shape[1]
    for j in range(n_slope):
        at = pl.multiple_of(pos[1 + j] * s_dev, s_dev)
        panel[:, pl.ds(at, s_dev)] = pieces[j][...]
    gram = lax.dot_general(
        panel[...], panel[...], (((1,), (1,)), ((), ())), preferred_element_type=F32
    )
    r = lax.broadcasted_iota(jnp.int32, (width, width), 0)
    c = lax.broadcasted_iota(jnp.int32, (width, width), 1)
    u_ref[...] = gram / float(total_rows) + jnp.where(r == c, load_ref[...], 0.0)
    n_blocks = width // B

    def body(k, _):
        o = pl.multiple_of(k * B, B)
        upper, inv = factor_tile(u_ref[pl.ds(o, B), pl.ds(o, B)])
        for g in range(B // 8):
            u_ref[pl.ds(o + 8 * g, 8), pl.ds(o, B)] = upper[g]
            inverse[8 * g : 8 * g + 8, :] = inv[g]
        for kk in range(n_blocks - 1):

            @pl.when(k == kk)
            def _():
                r0 = (kk + 1) * B
                strip = jnp.dot(
                    inverse[...], u_ref[kk * B : r0, r0:], precision=HIGHEST, preferred_element_type=F32
                )
                u_ref[kk * B : r0, r0:] = strip
                u_ref[r0:, r0:] = u_ref[r0:, r0:] - lax.dot_general(
                    strip, strip, (((0,), (0,)), ((), ())), precision=HIGHEST, preferred_element_type=F32
                )

        return 0

    lax.fori_loop(0, n_blocks, body, 0)
    wide = rows.shape[0]
    first = pos[0] * block
    base = first // wide * wide
    rows[...] = u_ref[:, pl.ds(pl.multiple_of(base, wide), wide)].T
    own = rows[pl.ds(pl.multiple_of(first - base, 8), block), :]
    row_ids = first + lax.broadcasted_iota(jnp.int32, (block, width), 0)
    col_ids = lax.broadcasted_iota(jnp.int32, (block, width), 1)
    o_ref[...] = jnp.where(row_ids >= col_ids, own, 0.0)


def factor_rows(pieces, load_col, pos, block, total_rows):
    n_slope = len(pieces)
    width, s_dev = pieces[0].shape
    vmem = pl.BlockSpec(memory_space=pltpu.VMEM)
    return pl.pallas_call(
        functools.partial(factor_kernel, n_slope=n_slope, total_rows=total_rows, block=block),
        out_shape=jax.ShapeDtypeStruct((block, width), F32),
        in_specs=[pl.BlockSpec(memory_space=pltpu.SMEM)] + [vmem] * (n_slope + 1),
        out_specs=vmem,
        scratch_shapes=[
            pltpu.VMEM((width, n_slope * s_dev), BF16),
            pltpu.VMEM((width, width), F32),
            pltpu.VMEM((B, B), F32),
            pltpu.VMEM((max(block, 128), width), F32),
        ],
        cost_estimate=pl.CostEstimate(
            flops=2 * width * width * total_rows * 10, bytes_accessed=140 << 20, transcendentals=width
        ),
        compiler_params=pltpu.CompilerParams(vmem_limit_bytes=40 << 20),
    )(pos, *pieces, load_col)


def gram_kernel(pos, *refs, n_slope, total_rows):
    rows_in = refs[:n_slope]
    panel_in = refs[n_slope : 2 * n_slope]
    o_ref, left, right = refs[2 * n_slope :]
    s_dev = rows_in[0].shape[1]

    @pl.when(pl.program_id(0) == 0)
    def _():
        for j in range(n_slope):
            at = pl.multiple_of(pos[1 + j] * s_dev, s_dev)
            right[pl.ds(at, s_dev), :] = panel_in[j][...].T

    for j in range(n_slope):
        at = pl.multiple_of(pos[1 + j] * s_dev, s_dev)
        left[:, pl.ds(at, s_dev)] = rows_in[j][...]
    o_ref[...] = jnp.dot(left[...], right[...], preferred_element_type=F32) / float(total_rows)


def gram_rows(pieces, panel, pos, total_rows, tile=256):
    n_slope = len(pieces)
    n, s_dev = pieces[0].shape
    width = panel[0].shape[0]
    return pl.pallas_call(
        functools.partial(gram_kernel, n_slope=n_slope, total_rows=total_rows),
        out_shape=jax.ShapeDtypeStruct((n, width), F32),
        grid_spec=pltpu.PrefetchScalarGridSpec(
            num_scalar_prefetch=1,
            grid=(n // tile,),
            in_specs=[pl.BlockSpec((tile, s_dev), lambda i, *_: (i, 0))] * n_slope
            + [pl.BlockSpec((width, s_dev), lambda i, *_: (0, 0))] * n_slope,
            out_specs=pl.BlockSpec((tile, width), lambda i, *_: (i, 0)),
            scratch_shapes=[
                pltpu.VMEM((tile, n_slope * s_dev), BF16),
                pltpu.VMEM((n_slope * s_dev, width), BF16),
            ],
        ),
        cost_estimate=pl.CostEstimate(
            flops=2 * n * width * total_rows, bytes_accessed=4 * n * width + 2 * n * total_rows, transcendentals=0
        ),
        compiler_params=pltpu.CompilerParams(
            vmem_limit_bytes=40 << 20, dimension_semantics=("arbitrary",)
        ),
    )(pos, *pieces, *panel)


def local(frames, frame_scale, codes, assign, loads):
    f_dev, s_dev = frames.shape
    n_tm, n_slope, n_act = lax.axis_size("tm"), lax.axis_size("slope"), lax.axis_size("act")
    tm_pos, slope_pos, act_pos = lax.axis_index("tm"), lax.axis_index("slope"), lax.axis_index("act")
    total_frames = f_dev * n_tm
    total_rows = s_dev * n_slope
    block = PW // n_act
    n_y = n_slope // 2

    own_codes = codes[:PW]
    panel_codes = own_codes
    for r in range(1, n_act):
        sent = lax.ppermute(own_codes, "act", [(0, r)])
        panel_codes = jnp.where(act_pos == r, sent, panel_codes)
    scale_rows = frame_scale.astype(BF16).astype(F32).reshape(f_dev // LO, LO)
    sgn = (1 - 2 * parity_bits(lax.iota(jnp.int32, n_tm) & tm_pos)).astype(F32)

    def sum_tm(part):
        total = part.astype(F32)
        for r in range(1, n_tm):
            total = total + lax.ppermute(
                part, "tm", [(i, (i + r) % n_tm) for i in range(n_tm)]
            ).astype(F32)
        return (total * (1.0 / math.sqrt(total_frames))).astype(BF16)

    def gather_slopes(im):
        column = [im]
        for r in range(1, n_y):
            column.append(
                lax.ppermute(
                    im,
                    "slope",
                    [(2 * y + k, 2 * ((y + r) % n_y) + k) for y in range(n_y) for k in range(2)],
                )
            )
        swap = [(i, i ^ 1) for i in range(n_slope)]
        return column + [lax.ppermute(v, "slope", swap) for v in column]

    y_pos, core_pos = slope_pos // 2, slope_pos % 2
    origin = [(y_pos - r + n_y) % n_y for r in range(n_y)]
    pos = jnp.stack(
        [act_pos] + [2 * y + core_pos for y in origin] + [2 * y + 1 - core_pos for y in origin]
    ).astype(jnp.int32)

    panel = gather_slopes(sum_tm(demod(frames, scale_rows, panel_codes, sgn)))
    mine = gather_slopes(sum_tm(demod(frames, scale_rows, codes, sgn)))

    mirror_ids = lax.broadcasted_iota(jnp.int32, (NDM, PW), 0)
    load_col = jnp.sum(jnp.where(assign[None, :] == mirror_ids, loads[:, None], 0.0), axis=0)
    factor = factor_rows(panel, load_col[None, :], pos, block, total_rows)
    gram_panel = gram_rows(mine, panel, pos, total_rows)
    return (gram_panel, factor)


def solution(mesh):
    return jax.shard_map(
        local,
        mesh=mesh,
        in_specs=(P("tm", "slope"), P("tm"), P("act"), P(), P()),
        out_specs=(P("act", None), P("act", None)),
        check_vma=False,
    )
```

```python
import functools
import math

import jax
import jax.numpy as jnp
from jax import lax
from jax.experimental import pallas as pl
from jax.experimental.pallas import tpu as pltpu
from jax.sharding import PartitionSpec as P

PW = 1024
NDM = 3
F32 = jnp.float32
BF16 = jnp.bfloat16
LO = 256
B = 128
HIGHEST = lax.Precision.HIGHEST


def parity_bits(values):
    for shift_by in (16, 8, 4, 2, 1):
        values = jnp.bitwise_xor(values, jnp.right_shift(values, shift_by))
    return jnp.bitwise_and(values, 1)


ANY = pl.BlockSpec(memory_space=pl.ANY)
VMEM = pl.BlockSpec(memory_space=pltpu.VMEM)
SMEM = pl.BlockSpec(memory_space=pltpu.SMEM)
HBM = pl.BlockSpec(memory_space=pltpu.HBM)


def params(mib):
    return pltpu.CompilerParams(vmem_limit_bytes=mib << 20)


def cost(elements):
    return pl.CostEstimate(flops=0, bytes_accessed=elements, transcendentals=0)


def transform_kernel(sgn, x_ref, w_ref, tab, had, buf, sems, *, n_hi, n_top, parts):
    s = x_ref.shape[1]
    per = n_hi // parts
    copies = [
        pltpu.make_async_copy(
            x_ref.at[pl.ds(p * per * LO, per * LO), :], buf.at[pl.ds(p * per * LO, per * LO), :], sems.at[p]
        )
        for p in range(parts)
    ]
    for copy in copies:
        copy.start()
    r = lax.broadcasted_iota(jnp.int32, (LO, LO), 0)
    c = lax.broadcasted_iota(jnp.int32, (LO, LO), 1)
    had[...] = (1 - 2 * parity_bits(r & c)).astype(F32)
    for p in range(parts):
        copies[p].wait()
        for k in range(p * per, (p + 1) * per):
            weights = (had[...] * w_ref[k : k + 1, :]).astype(BF16)
            tab[k * LO : (k + 1) * LO, :] = jnp.dot(
                weights, buf[k * LO : (k + 1) * LO, :], preferred_element_type=F32
            )

    def column(t, _):
        row = pl.multiple_of(t * 8, 8)
        for l in range(s // 128):
            lanes = slice(l * 128, (l + 1) * 128)
            v = [tab[pl.ds(h * LO + row, 8), lanes] for h in range(n_hi)]
            step = 1
            while step < n_hi:
                for a in range(n_hi):
                    if not a & step:
                        v[a], v[a + step] = v[a] + v[a + step], v[a] - v[a + step]
                step *= 2
            for h in range(n_hi):
                tab[pl.ds(h * LO + row, 8), lanes] = v[h]
                for j in range(1, n_top):
                    tab[pl.ds((j * n_hi + h) * LO + row, 8), lanes] = v[h] * sgn[j]
        return 0

    lax.fori_loop(0, LO // 8, column, 0)


def transform(frames, scale_rows, sgn):
    f, s = frames.shape
    n_hi, n_top = f // LO, sgn.shape[0]
    parts = 8
    return pl.pallas_call(
        functools.partial(transform_kernel, n_hi=n_hi, n_top=n_top, parts=parts),
        out_shape=jax.ShapeDtypeStruct((n_top * f, s), F32),
        in_specs=[SMEM, HBM, VMEM],
        out_specs=VMEM,
        scratch_shapes=[
            pltpu.VMEM((LO, LO), F32),
            pltpu.VMEM((f, s), BF16),
            pltpu.SemaphoreType.DMA((parts,)),
        ],
        cost_estimate=cost(f * s),
        compiler_params=params(24),
    )(sgn, frames, scale_rows)


def gather_kernel(codes, tab, *refs, base, group, n_dep):
    for o_ref in refs[n_dep:]:

        def some(t, _, o_ref=o_ref, base=base):
            at = pl.multiple_of(t * group, group)
            rows = [tab[pl.ds(codes[base + at + m], 1), :] for m in range(group)]
            o_ref[pl.ds(at, group), :] = jnp.concatenate(rows, axis=0).astype(BF16)
            return 0

        lax.fori_loop(0, o_ref.shape[0] // group, some, 0)
        base += o_ref.shape[0]


def gather(table, codes, base, sizes, deps=(), group=16):
    s = table.shape[1]
    return pl.pallas_call(
        functools.partial(gather_kernel, base=base, group=group, n_dep=len(deps)),
        out_shape=[jax.ShapeDtypeStruct((n, s), BF16) for n in sizes],
        in_specs=[SMEM, VMEM] + [ANY] * len(deps),
        out_specs=[VMEM] * len(sizes),
        cost_estimate=cost(sum(sizes) * s),
        compiler_params=params(20),
    )(codes, table, *deps)


def pick_kernel(act, *refs):
    picked = refs[0][...]
    for r, ref in enumerate(refs[1:-1], 1):
        picked = jnp.where(act[0] == r, ref[...], picked)
    refs[-1][...] = picked


def pick(candidates, act_pos):
    n = candidates[0].shape[0]
    return pl.pallas_call(
        pick_kernel,
        out_shape=jax.ShapeDtypeStruct((n // 128, 128), jnp.int32),
        in_specs=[SMEM] + [VMEM] * len(candidates),
        out_specs=VMEM,
        cost_estimate=cost(n),
        compiler_params=params(2),
    )(act_pos.reshape(1), *[c.reshape(n // 128, 128) for c in candidates]).reshape(n)


def combine_kernel(*refs, n, scale, skip):
    total = refs[0][...].astype(F32)
    for r in refs[1:n]:
        total = total + r[...].astype(F32)
    refs[n + skip][...] = (total * scale).astype(BF16)


def combine(parts, scale, passing=(), deps=()):
    n = len(parts)
    out = pl.pallas_call(
        functools.partial(combine_kernel, n=n, scale=scale, skip=len(passing) + len(deps)),
        out_shape=[jax.ShapeDtypeStruct(parts[0].shape, BF16)]
        + [jax.ShapeDtypeStruct(p.shape, p.dtype) for p in passing],
        in_specs=[VMEM] * n + [ANY] * (len(passing) + len(deps)),
        out_specs=[VMEM] + [ANY] * len(passing),
        input_output_aliases={n + i: 1 + i for i in range(len(passing))},
        cost_estimate=cost(parts[0].size),
        compiler_params=params(3),
    )(*parts, *passing, *deps)
    return out[0], list(out[1:])


def gate_kernel(*refs):
    pass


def gate(passing, dep):
    return list(
        pl.pallas_call(
            gate_kernel,
            out_shape=[jax.ShapeDtypeStruct(p.shape, p.dtype) for p in passing],
            in_specs=[ANY] * (len(passing) + 1),
            out_specs=[ANY] * len(passing),
            input_output_aliases={i: i for i in range(len(passing))},
            cost_estimate=cost(1024),
            compiler_params=params(1),
        )(*passing, dep)
    )


def across(v, lane):
    return jnp.broadcast_to(v[:, lane : lane + 1], (8, 128))


def down(v, row):
    return jnp.broadcast_to(v[row : row + 1, :], (8, 128))


def factor_tile(tile):
    lanes = lax.broadcasted_iota(jnp.int32, (8, 128), 1)
    subs = lax.broadcasted_iota(jnp.int32, (8, 128), 0)
    n = B // 8
    m = [tile[8 * g : 8 * g + 8, :] for g in range(n)]
    e = [jnp.where(lanes == subs + 8 * g, 1.0, 0.0).astype(F32) for g in range(n)]
    upper, inverse = [], []
    for q in range(n):
        cols = [across(m[q], 8 * q + j) for j in range(8)]
        s = {(i, j): down(cols[j], i) for j in range(8) for i in range(j, 8)}
        r = [down(m[q], i) for i in range(8)]
        t = [down(e[q], i) for i in range(8)]
        if q + 1 < n:
            c = [across(m[q + 1], 8 * q + j) for j in range(8)]
            m_next, e_next = m[q + 1], e[q + 1]
        far = {g: [across(m[g], 8 * q + j) for j in range(8)] for g in range(q + 2, n)}
        inv, u, w = [], [], []
        for j in range(8):
            root = lax.rsqrt(s[j, j])
            inv.append(root)
            l = {i: s[i, j] * root for i in range(j + 1, 8)}
            for i in range(j + 1, 8):
                for k in range(j + 1, i + 1):
                    s[i, k] = s[i, k] - l[i] * l[k]
                s[i, j] = l[i]
            u.append(r[j] * root)
            w.append(t[j] * root)
            for i in range(j + 1, 8):
                r[i] = r[i] - l[i] * u[j]
                t[i] = t[i] - l[i] * w[j]
            if q + 1 < n:
                lb = c[j] * root
                for k in range(j + 1, 8):
                    c[k] = c[k] - lb * l[k]
                m_next = m_next - lb * u[j]
                e_next = e_next - lb * w[j]
        u_rows, w_rows = u[0], w[0]
        for j in range(1, 8):
            u_rows = jnp.where(subs == j, u[j], u_rows)
            w_rows = jnp.where(subs == j, w[j], w_rows)
        upper.append(jnp.where(lanes >= subs + 8 * q, u_rows, 0.0))
        inverse.append(w_rows)
        if q + 1 < n:
            m[q + 1], e[q + 1] = m_next, e_next
        if q + 2 < n:
            ug, wg = [None] * 8, [None] * 8
            for j in reversed(range(8)):
                a, b = u[j], w[j]
                for i in range(j + 1, 8):
                    a = a - s[i, j] * ug[i]
                    b = b - s[i, j] * wg[i]
                ug[j], wg[j] = a * inv[j], b * inv[j]
            for g in range(q + 2, n):
                for j in range(8):
                    m[g] = m[g] - far[g][j] * ug[j]
                    e[g] = e[g] - far[g][j] * wg[j]
    return upper, inverse


def join(pieces, out, pos):
    s_dev = pieces[0].shape[1]
    for j, piece in enumerate(pieces):
        out[:, pl.ds(pl.multiple_of(pos[1 + j] * s_dev, s_dev), s_dev)] = piece[...]


def against(left, right):
    return lax.dot_general(left, right, (((1,), (1,)), ((), ())), preferred_element_type=F32)


def on_diagonal(assign, loads):
    n = assign.shape[1]
    load = jnp.zeros((1, n), F32)
    for m in range(NDM):
        load = jnp.where(assign == m, loads[m], load)
    r = lax.broadcasted_iota(jnp.int32, (n, n), 0)
    c = lax.broadcasted_iota(jnp.int32, (n, n), 1)
    return jnp.where(r == c, load, 0.0)


def factor_block(u_ref, inverse, k):
    o = pl.multiple_of(k * B, B)
    upper, inv = factor_tile(u_ref[pl.ds(o, B), pl.ds(o, B)])
    for g in range(B // 8):
        u_ref[pl.ds(o + 8 * g, 8), pl.ds(o, B)] = upper[g]
        inverse[8 * g : 8 * g + 8, :] = inv[g]


def eliminate(u_ref, inverse, k, start):
    top = slice(k * B, (k + 1) * B)
    strip = jnp.dot(inverse, u_ref[top, start:], precision=HIGHEST, preferred_element_type=F32)
    u_ref[top, start:] = strip
    return strip


def trailing(u_ref, k, rows, cols):
    top = slice(k * B, (k + 1) * B)
    u_ref[rows, cols] = u_ref[rows, cols] - lax.dot_general(
        u_ref[top, rows],
        u_ref[top, cols],
        (((0,), (0,)), ((), ())),
        precision=HIGHEST,
        preferred_element_type=F32,
    )


def factor_loop(u_ref, inverse, first, last):
    n = u_ref.shape[0]

    def body(k, _):
        factor_block(u_ref, inverse.at[k - first], k)
        for kk in range(first, last):
            if (kk + 1) * B < n:

                @pl.when(k == kk)
                def _():
                    r0 = (kk + 1) * B
                    eliminate(u_ref, inverse[kk - first], kk, r0)
                    trailing(u_ref, kk, slice(r0, n), slice(r0, n))

        return 0

    lax.fori_loop(first, last, body, 0)


def head_kernel(pos, loads, assign, *refs, n_slope, total_rows, n_dep):
    pieces = refs[:n_slope]
    left, u_ref, inverse = refs[n_slope + n_dep :]
    join(pieces, left, pos)
    n = u_ref.shape[0]
    u_ref[...] = against(left[...], left[...]) / float(total_rows) + on_diagonal(assign[:, :n], loads)
    factor_loop(u_ref, inverse, 0, u_ref.shape[0] // B)


def factor_head(pieces, loads, assign, pos, total_rows, deps=()):
    n_slope = len(pieces)
    n = pieces[0].shape[0]
    return pl.pallas_call(
        functools.partial(head_kernel, n_slope=n_slope, total_rows=total_rows, n_dep=len(deps)),
        out_shape=[
            jax.ShapeDtypeStruct((n, total_rows), BF16),
            jax.ShapeDtypeStruct((n, n), F32),
            jax.ShapeDtypeStruct((n // B, B, B), F32),
        ],
        in_specs=[SMEM] * 2 + [VMEM] * (n_slope + 1) + [ANY] * len(deps),
        out_specs=[VMEM] * 3,
        cost_estimate=cost(1 << 20),
        compiler_params=params(18),
    )(pos, loads, assign, *pieces, *deps)


def middle_kernel(pos, loads, assign, *refs, n_slope, total_rows, n_dep, last):
    pieces = refs[:n_slope]
    left0, u0, inv0 = refs[n_slope : n_slope + 3]
    right, u_ref, left1, inverse = refs[n_slope + 3 + n_dep :]
    join(pieces, left1, pos)
    h, n = u0.shape[0], u_ref.shape[0]
    right[:, :h] = left0[...].T
    right[:, h:] = left1[...].T
    u_ref[:h, :h] = u0[...]
    u_ref[:h, h:] = jnp.dot(left0[...], right[:, h:], preferred_element_type=F32) / float(total_rows)
    u_ref[h:, h:] = jnp.dot(left1[...], right[:, h:], preferred_element_type=F32) / float(
        total_rows
    ) + on_diagonal(assign[:, h:], loads)
    for k in range(h // B):
        eliminate(u_ref, inv0[k], k, h)
        if (k + 1) * B < h:
            trailing(u_ref, k, slice((k + 1) * B, h), slice(h, n))
    u_ref[h:, h:] = u_ref[h:, h:] - lax.dot_general(
        u_ref[:h, h:],
        u_ref[:h, h:],
        (((0,), (0,)), ((), ())),
        precision=HIGHEST,
        preferred_element_type=F32,
    )
    factor_loop(u_ref, inverse, h // B, last)


def factor_middle(pieces, loads, assign, head, pos, total_rows, last, deps=()):
    n_slope = len(pieces)
    left0, u0, inv0 = head
    n = pieces[0].shape[0] + u0.shape[0]
    return pl.pallas_call(
        functools.partial(
            middle_kernel, n_slope=n_slope, total_rows=total_rows, n_dep=len(deps), last=last
        ),
        out_shape=[jax.ShapeDtypeStruct((total_rows, n), BF16), jax.ShapeDtypeStruct((n, n), F32)],
        in_specs=[SMEM] * 2 + [VMEM] * (n_slope + 4) + [ANY] * len(deps),
        out_specs=[VMEM] * 2,
        scratch_shapes=[
            pltpu.VMEM((pieces[0].shape[0], total_rows), BF16),
            pltpu.VMEM((last - u0.shape[0] // B, B, B), F32),
        ],
        cost_estimate=cost(1 << 20),
        compiler_params=params(18),
    )(pos, loads, assign, *pieces, left0, u0, inv0, *deps)


def tail_kernel(pos, u_in, *refs, first, last, n_dep):
    u_ref, inverse = refs[n_dep:]
    factor_loop(u_ref, inverse, first, last)


def factor_more(u, pos, first, last, deps=()):
    return pl.pallas_call(
        functools.partial(tail_kernel, first=first, last=last, n_dep=len(deps)),
        out_shape=jax.ShapeDtypeStruct(u.shape, F32),
        in_specs=[SMEM, VMEM] + [ANY] * len(deps),
        out_specs=VMEM,
        scratch_shapes=[pltpu.VMEM((last - first, B, B), F32)],
        input_output_aliases={1: 0},
        cost_estimate=cost(1 << 20),
        compiler_params=params(18),
    )(pos, u, *deps)


def rows_kernel(pos, u_ref, *refs, block, n_dep):
    o_ref, rows = refs[n_dep:]
    width = u_ref.shape[1]
    wide = rows.shape[0]
    first = pos[0] * block
    base = first // wide * wide
    rows[...] = u_ref[:, pl.ds(pl.multiple_of(base, wide), wide)].T
    own = rows[pl.ds(pl.multiple_of(first - base, 8), block), :]
    row_ids = first + lax.broadcasted_iota(jnp.int32, (block, width), 0)
    col_ids = lax.broadcasted_iota(jnp.int32, (block, width), 1)
    o_ref[...] = jnp.where(row_ids >= col_ids, own, 0.0)


def own_rows(u, pos, block, deps=()):
    width = u.shape[1]
    return pl.pallas_call(
        functools.partial(rows_kernel, block=block, n_dep=len(deps)),
        out_shape=jax.ShapeDtypeStruct((block, width), F32),
        in_specs=[SMEM, VMEM] + [ANY] * len(deps),
        out_specs=VMEM,
        scratch_shapes=[pltpu.VMEM((max(block, 128), width), F32)],
        cost_estimate=cost(block * width),
        compiler_params=params(10),
    )(pos, u, *deps)


def gram_kernel(pos, *refs, n_slope, total_rows, n_dep):
    rows_in = refs[:n_slope]
    right = refs[n_slope]
    o_ref, left = refs[n_slope + 1 + n_dep :]
    join(rows_in, left, pos)
    o_ref[...] = jnp.dot(left[...], right[...], preferred_element_type=F32) / float(total_rows)


def gram_rows(pieces, right, pos, out, at, total, deps=(), tile=256):
    n_slope = len(pieces)
    n, s_dev = pieces[0].shape
    total_rows, width = right.shape
    deps = ((out,) if out is not None else ()) + tuple(deps)
    return pl.pallas_call(
        functools.partial(gram_kernel, n_slope=n_slope, total_rows=total_rows, n_dep=len(deps)),
        out_shape=jax.ShapeDtypeStruct((total, width), F32),
        grid_spec=pltpu.PrefetchScalarGridSpec(
            num_scalar_prefetch=1,
            grid=(n // tile,),
            in_specs=[pl.BlockSpec((tile, s_dev), lambda i, *_: (i, 0))] * n_slope
            + [pl.BlockSpec((total_rows, width), lambda i, *_: (0, 0))]
            + [ANY] * len(deps),
            out_specs=pl.BlockSpec((tile, width), lambda i, *_: (i + at // tile, 0)),
            scratch_shapes=[pltpu.VMEM((tile, n_slope * s_dev), BF16)],
        ),
        input_output_aliases={} if out is None else {2 + n_slope: 0},
        cost_estimate=cost(n * width),
        compiler_params=pltpu.CompilerParams(
            vmem_limit_bytes=16 << 20, dimension_semantics=("arbitrary",)
        ),
    )(pos, *pieces, right, *deps)


def local(frames, frame_scale, codes, assign, loads):
    f_dev, s_dev = frames.shape
    a_dev = codes.shape[0]
    n_tm, n_slope, n_act = lax.axis_size("tm"), lax.axis_size("slope"), lax.axis_size("act")
    tm_pos, slope_pos, act_pos = lax.axis_index("tm"), lax.axis_index("slope"), lax.axis_index("act")
    scale = 1.0 / math.sqrt(f_dev * n_tm)
    total_rows = s_dev * n_slope
    block = PW // n_act
    n_y = n_slope // 2
    head = 256
    chunks = max(1, min(4, a_dev // 1024))
    chunk = a_dev // chunks

    own_codes = codes[:PW]
    panel_codes = pick(
        [own_codes] + [lax.ppermute(own_codes, "act", [(0, r)]) for r in range(1, n_act)], act_pos
    )
    scale_rows = frame_scale.astype(BF16).astype(F32).reshape(f_dev // LO, LO)
    sgn = (1 - 2 * parity_bits(lax.iota(jnp.int32, n_tm) & tm_pos)).astype(F32)
    y_pos, core_pos = slope_pos // 2, slope_pos % 2
    origin = [(y_pos - r + n_y) % n_y for r in range(n_y)]
    pos = jnp.stack(
        [act_pos] + [2 * y + core_pos for y in origin] + [2 * y + 1 - core_pos for y in origin]
    ).astype(jnp.int32)
    assign = assign[None, :]

    def over_tm(part):
        return [part] + [
            lax.ppermute(part, "tm", [(i, (i + r) % n_tm) for i in range(n_tm)]) for r in range(1, n_tm)
        ]

    def over_y(im):
        return [im] + [
            lax.ppermute(
                im,
                "slope",
                [(2 * y + k, 2 * ((y + r) % n_y) + k) for y in range(n_y) for k in range(2)],
            )
            for r in range(1, n_y)
        ]

    def over_core(column):
        swap = [(i, i ^ 1) for i in range(n_slope)]
        return [lax.ppermute(v, "slope", swap) for v in column]

    class Part:
        def __init__(self, part):
            self.part = part
            self.over_tm = over_tm(part)

        def reduce(self, before=None, deps=()):
            passing = before.column[1:] if before else []
            im, passed = combine(self.over_tm, scale, passing, deps)
            self.column = over_y(im)
            self.own = over_core([im])
            self.im = im
            if before:
                before.arrive(passed)

        def arrive(self, passed):
            self.column = [self.im] + passed
            self.pieces = self.column + self.own + over_core(passed)

    table = transform(frames, scale_rows, sgn)
    p0, p1 = [Part(p) for p in gather(table, panel_codes, 0, [head, PW - head])]
    mine = []
    for c in range(chunks):
        last = mine[-1].part if mine else p1.part
        mine.append(Part(gather(table, codes, c * chunk, [chunk], deps=(last,))[0]))
    p0.reduce(deps=(mine[-1].part,))
    p1.reduce(before=p0, deps=(p0.im,))
    first = factor_head(p0.pieces, loads, assign, pos, total_rows, deps=(p1.im,))
    n_blocks = PW // B
    waiting = [p1]
    left_over = list(mine)

    def slot(dep):
        if left_over:
            part = left_over.pop(0)
            part.reduce(before=waiting.pop(), deps=(dep,))
            waiting.append(part)
            return (part.im,)
        return ()

    h = head // B
    deps = slot(first[2])
    right, u = factor_middle(p1.pieces, loads, assign, first, pos, total_rows, h + 1, deps=deps)
    for k in range(h + 1, n_blocks - 1):
        deps = slot(u)
        u = factor_more(u, pos, k, k + 1, deps=deps)
    for part in waiting:
        part.arrive(gate(part.column[1:], u))
    u = factor_more(u, pos, n_blocks - 1, n_blocks)
    factor = own_rows(u, pos, block)
    out = None
    for c in range(chunks):
        out = gram_rows(mine[c].pieces, right, pos, out, c * chunk, a_dev, deps=(u,))
    return (out, factor)


def solution(mesh):
    return jax.shard_map(
        local,
        mesh=mesh,
        in_specs=(P("tm", "slope"), P("tm"), P("act"), P(), P()),
        out_specs=(P("act", None), P("act", None)),
        check_vma=False,
    )
```

```python
import functools
import math

import jax
import jax.numpy as jnp
from jax import lax
from jax.experimental import pallas as pl
from jax.experimental.pallas import tpu as pltpu
from jax.sharding import PartitionSpec as P

PW = 1024
NDM = 3
F32 = jnp.float32
BF16 = jnp.bfloat16
TOKEN = jax.ShapeDtypeStruct((8, 128), F32)
LO = 256
B = 128
NEAR = 3
HIGHEST = lax.Precision.HIGHEST


def parity_bits(values):
    for shift_by in (16, 8, 4, 2, 1):
        values = jnp.bitwise_xor(values, jnp.right_shift(values, shift_by))
    return jnp.bitwise_and(values, 1)


ANY = pl.BlockSpec(memory_space=pl.ANY)
VMEM = pl.BlockSpec(memory_space=pltpu.VMEM)
SMEM = pl.BlockSpec(memory_space=pltpu.SMEM)
HBM = pl.BlockSpec(memory_space=pltpu.HBM)


def params(mib):
    return pltpu.CompilerParams(vmem_limit_bytes=mib << 20)


def cost(elements):
    return pl.CostEstimate(flops=0, bytes_accessed=elements, transcendentals=0)


def transform_kernel(sgn, x_ref, w_ref, tab, had, buf, sems, *, n_hi, n_top, parts):
    s = x_ref.shape[1]
    per = n_hi // parts
    copies = [
        pltpu.make_async_copy(
            x_ref.at[pl.ds(p * per * LO, per * LO), :], buf.at[pl.ds(p * per * LO, per * LO), :], sems.at[p]
        )
        for p in range(parts)
    ]
    for copy in copies:
        copy.start()
    r = lax.broadcasted_iota(jnp.int32, (LO, LO), 0)
    c = lax.broadcasted_iota(jnp.int32, (LO, LO), 1)
    had[...] = (1 - 2 * parity_bits(r & c)).astype(F32)
    for p in range(parts):
        copies[p].wait()
        for k in range(p * per, (p + 1) * per):
            weights = (had[...] * w_ref[k : k + 1, :]).astype(BF16)
            tab[k * LO : (k + 1) * LO, :] = jnp.dot(
                weights, buf[k * LO : (k + 1) * LO, :], preferred_element_type=F32
            )

    def column(t, _):
        row = pl.multiple_of(t * 8, 8)
        for l in range(s // 128):
            lanes = slice(l * 128, (l + 1) * 128)
            v = [tab[pl.ds(h * LO + row, 8), lanes] for h in range(n_hi)]
            step = 1
            while step < n_hi:
                for a in range(n_hi):
                    if not a & step:
                        v[a], v[a + step] = v[a] + v[a + step], v[a] - v[a + step]
                step *= 2
            for h in range(n_hi):
                tab[pl.ds(h * LO + row, 8), lanes] = v[h]
                for j in range(1, n_top):
                    tab[pl.ds((j * n_hi + h) * LO + row, 8), lanes] = v[h] * sgn[j]
        return 0

    lax.fori_loop(0, LO // 8, column, 0)


def transform(frames, scale_rows, sgn):
    f, s = frames.shape
    n_hi, n_top = f // LO, sgn.shape[0]
    parts = 8
    return pl.pallas_call(
        functools.partial(transform_kernel, n_hi=n_hi, n_top=n_top, parts=parts),
        out_shape=jax.ShapeDtypeStruct((n_top * f, s), F32),
        in_specs=[SMEM, HBM, VMEM],
        out_specs=VMEM,
        scratch_shapes=[
            pltpu.VMEM((LO, LO), F32),
            pltpu.VMEM((f, s), BF16),
            pltpu.SemaphoreType.DMA((parts,)),
        ],
        cost_estimate=cost(f * s),
        compiler_params=params(24),
    )(sgn, pltpu.with_memory_space_constraint(frames, pltpu.HBM), scale_rows)


def gather_kernel(codes, tab, *refs, base, group, n_dep, n_out):
    for o_ref in refs[n_dep : n_dep + n_out]:

        def some(t, _, o_ref=o_ref, base=base):
            at = pl.multiple_of(t * group, group)
            rows = [tab[pl.ds(codes[base + at + m], 1), :] for m in range(group)]
            o_ref[pl.ds(at, group), :] = jnp.concatenate(rows, axis=0).astype(BF16)
            return 0

        lax.fori_loop(0, o_ref.shape[0] // group, some, 0)
        base += o_ref.shape[0]


def gather(table, codes, base, n, deps=(), passing=(), group=16):
    s = table.shape[1]
    return pl.pallas_call(
        functools.partial(
            gather_kernel, base=base, group=group, n_dep=len(deps) + len(passing), n_out=1
        ),
        out_shape=[jax.ShapeDtypeStruct((n, s), BF16)]
        + [jax.ShapeDtypeStruct(v.shape, v.dtype) for v in passing],
        in_specs=[SMEM, VMEM] + [ANY] * (len(passing) + len(deps)),
        out_specs=[VMEM] + [ANY] * len(passing),
        input_output_aliases={2 + i: 1 + i for i in range(len(passing))},
        cost_estimate=cost(n * s),
        compiler_params=params(20),
    )(codes, table, *passing, *deps)


def pick_kernel(act, own, sent, o_ref, *, reach):
    o_ref[...] = jnp.where(act[0] >= reach, sent[...], own[...])


def pick(own, sent, act_pos, reach):
    n = own.shape[0]
    return pl.pallas_call(
        functools.partial(pick_kernel, reach=reach),
        out_shape=jax.ShapeDtypeStruct((n // 128, 128), jnp.int32),
        in_specs=[SMEM, VMEM, VMEM],
        out_specs=VMEM,
        cost_estimate=cost(n),
        compiler_params=params(2),
    )(act_pos.reshape(1), own.reshape(n // 128, 128), sent.reshape(n // 128, 128)).reshape(n)


def combine_kernel(*refs, n, columns, split, scale, n_dep):
    outs = refs[n + sum(columns) + n_dep :]
    for k in range(split if n else 0):
        rows = slice(k * outs[k].shape[0], (k + 1) * outs[k].shape[0])
        total = refs[0][rows, :].astype(F32)
        for r in refs[1:n]:
            total = total + r[rows, :].astype(F32)
        outs[k][...] = (total * scale).astype(BF16)
    at = n
    for length, out in zip(columns, outs[split if n else 0 :]):
        for j in range(length):
            rows = refs[at].shape[0]
            out[j * rows : (j + 1) * rows, :] = refs[at][...]
            at += 1


def combine(parts, columns, scale, deps=(), split=1, passing=()):
    shapes = []
    if parts:
        n, s = parts[0].shape
        shapes += [jax.ShapeDtypeStruct((n // split, s), BF16)] * split
    for column in columns:
        shapes.append(jax.ShapeDtypeStruct((len(column) * column[0].shape[0], column[0].shape[1]), BF16))
    arrays = list(parts) + [v for column in columns for v in column]
    out = pl.pallas_call(
        functools.partial(
            combine_kernel,
            n=len(parts),
            columns=[len(column) for column in columns],
            split=split,
            scale=scale,
            n_dep=len(passing) + len(deps),
        ),
        out_shape=shapes + [jax.ShapeDtypeStruct(v.shape, v.dtype) for v in passing],
        in_specs=[VMEM] * len(arrays) + [ANY] * (len(passing) + len(deps)),
        out_specs=[VMEM] * len(shapes) + [ANY] * len(passing),
        input_output_aliases={len(arrays) + i: len(shapes) + i for i in range(len(passing))},
        cost_estimate=cost(shapes[0].size),
        compiler_params=params(12),
    )(*arrays, *passing, *deps)
    n = split if parts else 0
    return list(out[:n]), list(out[n : len(shapes)]), list(out[len(shapes) :])


def across(v, lane):
    return jnp.broadcast_to(v[:, lane : lane + 1], (8, 128))


def down(v, row):
    return jnp.broadcast_to(v[row : row + 1, :], (8, 128))


def factor_tile(tile):
    lanes = lax.broadcasted_iota(jnp.int32, (8, 128), 1)
    subs = lax.broadcasted_iota(jnp.int32, (8, 128), 0)
    n = B // 8
    m = [tile[8 * g : 8 * g + 8, :] for g in range(n)]
    d = [across(m[0], k) for k in range(8)]
    upper, inverse = [], []
    for q in range(n):
        o = 8 * q
        done = lanes < o + 8
        here = done & (lanes >= o)
        s = {(i, j): down(d[j], i) for j in range(8) for i in range(j, 8)}
        e = jnp.where(lanes < o, m[q], jnp.where(lanes == subs + o, 1.0, 0.0))
        r = [down(m[q], i) for i in range(8)]
        t = [down(e, i) for i in range(8)]
        near = range(q + 1, min(q + 1 + NEAR, n))
        far = range(q + 1 + NEAR, n)
        c = {g: [across(m[g], o + j) for j in range(8)] for g in range(q + 1, n)}
        if q + 1 < n:
            d = [across(m[q + 1], o + 8 + k) for k in range(8)]
        for g in range(q + 1, n):
            m[g] = jnp.where(here, 0.0, m[g])
        root, u, w, z = [], [], [], []
        for j in range(8):
            root.append(lax.rsqrt(s[j, j]))
            for i in range(j + 1, 8):
                s[i, j] = s[i, j] * root[j]
            for i in range(j + 1, 8):
                for k in range(j + 1, i + 1):
                    s[i, k] = s[i, k] - s[i, j] * s[k, j]
            u.append(r[j] * root[j])
            w.append(t[j] * root[j])
            z.append(jnp.where(done, w[j], u[j]))
            for i in range(j + 1, 8):
                r[i] = r[i] - s[i, j] * u[j]
                t[i] = t[i] - s[i, j] * w[j]
            for g in near:
                column = c[g][j] * root[j]
                for k in range(j + 1, 8):
                    c[g][k] = c[g][k] - column * s[k, j]
                m[g] = m[g] - column * z[j]
                if g == q + 1:
                    for k in range(8):
                        d[k] = d[k] - column * down(column, k)
        u_rows, w_rows = u[0], w[0]
        for j in range(1, 8):
            u_rows = jnp.where(subs == j, u[j], u_rows)
            w_rows = jnp.where(subs == j, w[j], w_rows)
        upper.append(jnp.where(lanes >= subs + o, u_rows, 0.0))
        inverse.append(w_rows)
        if far:
            for j in reversed(range(8)):
                for i in range(j + 1, 8):
                    z[j] = z[j] - s[i, j] * z[i]
                z[j] = z[j] * root[j]
            for g in far:
                for j in range(8):
                    m[g] = m[g] - c[g][j] * z[j]
    return upper, inverse


def join(pair, out, pos, start=0, n=None):
    n_slope = pos.shape[0] - 1
    s_dev = pair[0].shape[1]
    size = pair[0].shape[0] * 2 // n_slope
    for j in range(n_slope):
        source, at = pair[j * 2 // n_slope], j % (n_slope // 2) * size + start
        out[:, pl.ds(pl.multiple_of(pos[1 + j] * s_dev, s_dev), s_dev)] = source[at : at + (n or size), :]


def against(left, right):
    return lax.dot_general(left, right, (((1,), (1,)), ((), ())), preferred_element_type=F32)


def on_diagonal(assign, loads):
    n = assign.shape[1]
    load = jnp.zeros((1, n), F32)
    for m in range(NDM):
        load = jnp.where(assign == m, loads[m], load)
    r = lax.broadcasted_iota(jnp.int32, (n, n), 0)
    c = lax.broadcasted_iota(jnp.int32, (n, n), 1)
    return jnp.where(r == c, load, 0.0)


def factor_block(u_ref, inverse, k):
    o = pl.multiple_of(k * B, B)
    upper, inv = factor_tile(u_ref[pl.ds(o, B), pl.ds(o, B)])
    for g in range(B // 8):
        u_ref[pl.ds(o + 8 * g, 8), pl.ds(o, B)] = upper[g]
        inverse[8 * g : 8 * g + 8, :] = inv[g]


def eliminate(u_ref, inverse, k, start):
    top = slice(k * B, (k + 1) * B)
    strip = jnp.dot(inverse, u_ref[top, start:], precision=HIGHEST, preferred_element_type=F32)
    u_ref[top, start:] = strip
    return strip


def trailing(u_ref, k, rows, cols):
    top = slice(k * B, (k + 1) * B)
    u_ref[rows, cols] = u_ref[rows, cols] - lax.dot_general(
        u_ref[top, rows],
        u_ref[top, cols],
        (((0,), (0,)), ((), ())),
        precision=HIGHEST,
        preferred_element_type=F32,
    )


def factor_loop(u_ref, inverse, first, last):
    n = u_ref.shape[0]

    def body(k, _):
        factor_block(u_ref, inverse.at[k - first], k)
        for kk in range(first, last):
            if (kk + 1) * B < n:

                @pl.when(k == kk)
                def _():
                    r0 = (kk + 1) * B
                    eliminate(u_ref, inverse[kk - first], kk, r0)
                    trailing(u_ref, kk, slice(r0, n), slice(r0, n))

        return 0

    lax.fori_loop(first, last, body, 0)


def head_kernel(pos, loads, assign, *refs, total_rows, n_dep):
    left, u_ref, inverse = refs[2 + n_dep :]
    join(refs[:2], left, pos)
    n = u_ref.shape[0]
    u_ref[...] = against(left[...], left[...]) * (1.0 / total_rows) + on_diagonal(assign[:, :n], loads)
    factor_loop(u_ref, inverse, 0, u_ref.shape[0] // B)


def factor_head(pieces, loads, assign, pos, total_rows, deps=()):
    n = pieces[0].shape[0] * pieces[0].shape[1] * 2 // total_rows
    return pl.pallas_call(
        functools.partial(head_kernel, total_rows=total_rows, n_dep=len(deps)),
        out_shape=[
            jax.ShapeDtypeStruct((n, total_rows), BF16),
            jax.ShapeDtypeStruct((n, n), F32),
            jax.ShapeDtypeStruct((n // B, B, B), F32),
        ],
        in_specs=[SMEM] * 2 + [VMEM] * 3 + [ANY] * len(deps),
        out_specs=[VMEM] * 3,
        cost_estimate=cost(1 << 20),
        compiler_params=params(18),
    )(pos, loads, assign, *pieces, *deps)


def middle_kernel(pos, loads, assign, *refs, total_rows, n_dep, last):
    left0, u0, inv0 = refs[2:5]
    right, u_ref, left1, inverse = refs[5 + n_dep :]
    join(refs[:2], left1, pos)
    h, n = u0.shape[0], u_ref.shape[0]
    right[:, :h] = left0[...].T
    right[:, h:] = left1[...].T
    u_ref[:h, :h] = u0[...]
    u_ref[:h, h:] = jnp.dot(left0[...], right[:, h:], preferred_element_type=F32) * (1.0 / total_rows)
    u_ref[h:, h:] = jnp.dot(left1[...], right[:, h:], preferred_element_type=F32) * (
        1.0 / total_rows
    ) + on_diagonal(assign[:, h:], loads)
    for k in range(h // B):
        eliminate(u_ref, inv0[k], k, h)
        if (k + 1) * B < h:
            trailing(u_ref, k, slice((k + 1) * B, h), slice(h, n))
    u_ref[h:, h:] = u_ref[h:, h:] - lax.dot_general(
        u_ref[:h, h:],
        u_ref[:h, h:],
        (((0,), (0,)), ((), ())),
        precision=HIGHEST,
        preferred_element_type=F32,
    )
    factor_loop(u_ref, inverse, h // B, last)


def factor_middle(pieces, loads, assign, head, pos, total_rows, last, deps=()):
    left0, u0, inv0 = head
    below = pieces[0].shape[0] * pieces[0].shape[1] * 2 // total_rows
    n = below + u0.shape[0]
    return pl.pallas_call(
        functools.partial(middle_kernel, total_rows=total_rows, n_dep=len(deps), last=last),
        out_shape=[jax.ShapeDtypeStruct((total_rows, n), BF16), jax.ShapeDtypeStruct((n, n), F32)],
        in_specs=[SMEM] * 2 + [VMEM] * 6 + [ANY] * len(deps),
        out_specs=[VMEM] * 2,
        scratch_shapes=[
            pltpu.VMEM((below, total_rows), BF16),
            pltpu.VMEM((last - u0.shape[0] // B, B, B), F32),
        ],
        cost_estimate=cost(1 << 20),
        compiler_params=params(18),
    )(pos, loads, assign, *pieces, left0, u0, inv0, *deps)


def tail_kernel(pos, u_in, *refs, first, last, n_dep):
    u_ref, token, inverse = refs[n_dep:]
    factor_loop(u_ref, inverse, first, last)
    token[...] = jnp.zeros_like(token)


def factor_more(u, pos, first, last, deps=()):
    return pl.pallas_call(
        functools.partial(tail_kernel, first=first, last=last, n_dep=len(deps)),
        out_shape=[jax.ShapeDtypeStruct(u.shape, F32), TOKEN],
        in_specs=[SMEM, VMEM] + [ANY] * len(deps),
        out_specs=[VMEM] * 2,
        scratch_shapes=[pltpu.VMEM((last - first, B, B), F32)],
        input_output_aliases={1: 0},
        cost_estimate=cost(1 << 20),
        compiler_params=params(18),
    )(pos, u, *deps)


def rows_kernel(pos, u_ref, *refs, block, n_dep):
    o_ref, rows = refs[n_dep:]
    width = u_ref.shape[1]
    wide = rows.shape[0]
    first = pos[0] * block
    base = first // wide * wide
    rows[...] = u_ref[:, pl.ds(pl.multiple_of(base, wide), wide)].T
    own = rows[pl.ds(pl.multiple_of(first - base, 8), block), :]
    row_ids = first + lax.broadcasted_iota(jnp.int32, (block, width), 0)
    col_ids = lax.broadcasted_iota(jnp.int32, (block, width), 1)
    o_ref[...] = jnp.where(row_ids >= col_ids, own, 0.0)


def own_rows(u, pos, block, deps=()):
    width = u.shape[1]
    return pl.pallas_call(
        functools.partial(rows_kernel, block=block, n_dep=len(deps)),
        out_shape=jax.ShapeDtypeStruct((block, width), F32),
        in_specs=[SMEM, VMEM] + [ANY] * len(deps),
        out_specs=VMEM,
        scratch_shapes=[pltpu.VMEM((max(block, 128), width), F32)],
        cost_estimate=cost(block * width),
        compiler_params=params(10),
    )(pos, u, *deps)


def gram_kernel(pos, *refs, n, total_rows, n_dep, at, tile):
    right = refs[2]
    o_ref, token, left, buf, sems = refs[3 + n_dep :]
    token[...] = jnp.zeros_like(token)
    copies = []
    for t in range(n // tile):
        join(refs[:2], left, pos, t * tile, tile)
        if t >= 2:
            copies[t - 2].wait()
        buf[t % 2] = jnp.dot(left[...], right[...], preferred_element_type=F32) * (1.0 / total_rows)
        copies.append(
            pltpu.make_async_copy(buf.at[t % 2], o_ref.at[pl.ds(at + t * tile, tile), :], sems.at[t % 2])
        )
        copies[-1].start()
    for copy in copies[-2:]:
        copy.wait()


def gram_rows(pieces, right, pos, out, at, total, deps=(), tile=512):
    total_rows, width = right.shape
    n = pieces[0].shape[0] * pieces[0].shape[1] * 2 // total_rows
    deps = ((out,) if out is not None else ()) + tuple(deps)
    return pl.pallas_call(
        functools.partial(
            gram_kernel, n=n, total_rows=total_rows, n_dep=len(deps), at=at, tile=tile
        ),
        out_shape=[jax.ShapeDtypeStruct((total, width), F32), TOKEN],
        in_specs=[SMEM] + [VMEM] * 3 + [ANY] * len(deps),
        out_specs=[HBM, VMEM],
        scratch_shapes=[
            pltpu.VMEM((tile, total_rows), BF16),
            pltpu.VMEM((2, tile, width), F32),
            pltpu.SemaphoreType.DMA((2,)),
        ],
        input_output_aliases={} if out is None else {4: 0},
        cost_estimate=cost(n * width),
        compiler_params=params(12),
    )(pos, *pieces, right, *deps)


def local(frames, frame_scale, codes, assign, loads):
    f_dev, s_dev = frames.shape
    a_dev = codes.shape[0]
    n_tm, n_slope, n_act = lax.axis_size("tm"), lax.axis_size("slope"), lax.axis_size("act")
    tm_pos, slope_pos, act_pos = lax.axis_index("tm"), lax.axis_index("slope"), lax.axis_index("act")
    scale = 1.0 / math.sqrt(f_dev * n_tm)
    total_rows = s_dev * n_slope
    block = PW // n_act
    n_y = n_slope // 2
    head = 256

    own_codes = codes[:PW]
    panel_codes = own_codes
    reach = 1
    while reach < n_act:
        sent = lax.ppermute(
            panel_codes, "act", [(i, i + reach) for i in range(min(reach, n_act - reach))]
        )
        panel_codes = pick(panel_codes, sent, act_pos, reach)
        reach *= 2
    scale_rows = frame_scale.astype(BF16).astype(F32).reshape(f_dev // LO, LO)
    sgn = (1 - 2 * parity_bits(lax.iota(jnp.int32, n_tm) & tm_pos)).astype(F32)
    y_pos, core_pos = slope_pos // 2, slope_pos % 2
    origin = [(y_pos - r + n_y) % n_y for r in range(n_y)]
    pos = jnp.stack(
        [act_pos] + [2 * y + core_pos for y in origin] + [2 * y + 1 - core_pos for y in origin]
    ).astype(jnp.int32)
    assign = assign[None, :]

    def over_tm(part):
        return [part] + [
            lax.ppermute(part, "tm", [(i, (i + r) % n_tm) for i in range(n_tm)]) for r in range(1, n_tm)
        ]

    def over_y(im):
        return [im] + [
            lax.ppermute(
                im,
                "slope",
                [(2 * y + k, 2 * ((y + r) % n_y) + k) for y in range(n_y) for k in range(2)],
            )
            for r in range(1, n_y)
        ]

    def over_core(column):
        return lax.ppermute(column, "slope", [(i, i ^ 1) for i in range(n_slope)])

    class Chunk:
        def __init__(self, im):
            self.column = over_y(im)

    def slot(parts=(), split=1, release=(), deps=(), passing=()):
        ims, columns, passed = combine(
            parts, [chunk.column for chunk in release], scale, deps, split, passing
        )
        for chunk, column in zip(release, columns):
            chunk.pieces = [column, over_core(column)]
        return [Chunk(im) for im in ims], (ims + columns)[0], passed

    table = transform(frames, scale_rows, sgn)
    several = a_dev >= 4096
    unit = a_dev // 4 if several else a_dev
    (p0,) = gather(table, panel_codes, 0, head)
    (p1,) = gather(table, panel_codes, head, PW - head, deps=(p0,))
    (m0,) = gather(table, codes, 0, unit, deps=(p1,))
    (p0,), dep, (p1,) = slot(over_tm(p0), deps=(m0,), passing=(p1,))
    p1 = over_tm(p1)
    if several:
        m1, m0 = gather(table, codes, unit, 2 * unit, deps=(dep,), passing=(m0,))
        m0 = over_tm(m0)
        m2, m1 = gather(table, codes, 3 * unit, unit, passing=(m1,))
        m1 = over_tm(m1)
        (p1,), dep, _ = slot(p1, release=[p0], deps=(m2,))
    else:
        m0 = over_tm(m0)
        (p1,), dep, _ = slot(p1, release=[p0])
    first = factor_head(p0.pieces, loads, assign, pos, total_rows, deps=(dep,))
    if several:
        chunks, dep, (m2,) = slot(m0, release=[p1], deps=(first[2],), passing=(m2,))
        m2 = over_tm(m2)
    else:
        chunks, dep, _ = slot(m0, release=[p1], deps=(first[2],))
    h, n_blocks = head // B, PW // B
    right, u = factor_middle(p1.pieces, loads, assign, first, pos, total_rows, h + 1, deps=(dep,))
    token = right
    out = None

    def more(k, dep):
        return factor_more(u, pos, k, k + 1, deps=(dep,))

    def gram(c, out, dep):
        return gram_rows(chunks[c].pieces, right, pos, out, c * unit, a_dev, deps=(dep,))

    u, token = more(h + 1, token)
    if several:
        new, token, _ = slot(m1, 2, release=chunks[:1], deps=(token,))
        chunks += new
    else:
        _, token, _ = slot(release=chunks, deps=(token,))
    u, token = more(h + 2, token)
    u, token = more(h + 3, token)
    if several:
        new, token, _ = slot(m2, release=chunks[1:2], deps=(token,))
        chunks += new
    for k in range(h + 4, n_blocks - 1):
        u, token = more(k, token)
    for c in range(2 if several else 0):
        out, token = gram(c, out, token)
    if several:
        _, token, _ = slot(release=chunks[2:3], deps=(token,))
    u, token = more(n_blocks - 1, token)
    factor = own_rows(u, pos, block)
    if several:
        out, token = gram(2, out, token)
        _, token, _ = slot(release=chunks[3:], deps=(token,))
    out, token = gram(len(chunks) - 1, out, token)
    return (out, factor)


def solution(mesh):
    return jax.shard_map(
        local,
        mesh=mesh,
        in_specs=(P("tm", "slope"), P("tm"), P("act"), P(), P()),
        out_specs=(P("act", None), P("act", None)),
        check_vma=False,
    )
```

```python
import functools
import math

import jax
import jax.numpy as jnp
from jax import lax
from jax.experimental import pallas as pl
from jax.experimental.pallas import tpu as pltpu
from jax.sharding import PartitionSpec as P

PW = 1024
NDM = 3
F32 = jnp.float32
BF16 = jnp.bfloat16
TOKEN = jax.ShapeDtypeStruct((8, 128), F32)
LO = 256
B = 128
NEAR = 3
HIGHEST = lax.Precision.HIGHEST


def parity_bits(values):
    for shift_by in (16, 8, 4, 2, 1):
        values = jnp.bitwise_xor(values, jnp.right_shift(values, shift_by))
    return jnp.bitwise_and(values, 1)


ANY = pl.BlockSpec(memory_space=pl.ANY)
VMEM = pl.BlockSpec(memory_space=pltpu.VMEM)
SMEM = pl.BlockSpec(memory_space=pltpu.SMEM)
HBM = pl.BlockSpec(memory_space=pltpu.HBM)


def params(mib):
    return pltpu.CompilerParams(vmem_limit_bytes=mib << 20)


def cost(elements):
    return pl.CostEstimate(flops=0, bytes_accessed=elements, transcendentals=0)


def transform_kernel(sgn, x_ref, w_ref, tab, had, buf, sems, *, n_hi, n_top, parts):
    s = x_ref.shape[1]
    per = n_hi // parts
    copies = [
        pltpu.make_async_copy(
            x_ref.at[pl.ds(p * per * LO, per * LO), :], buf.at[pl.ds(p * per * LO, per * LO), :], sems.at[p]
        )
        for p in range(parts)
    ]
    for copy in copies:
        copy.start()
    r = lax.broadcasted_iota(jnp.int32, (LO, LO), 0)
    c = lax.broadcasted_iota(jnp.int32, (LO, LO), 1)
    had[...] = (1 - 2 * parity_bits(r & c)).astype(F32)
    for p in range(parts):
        copies[p].wait()
        for k in range(p * per, (p + 1) * per):
            weights = (had[...] * w_ref[k : k + 1, :]).astype(BF16)
            tab[k * LO : (k + 1) * LO, :] = jnp.dot(
                weights, buf[k * LO : (k + 1) * LO, :], preferred_element_type=F32
            )

    def column(t, _):
        row = pl.multiple_of(t * 8, 8)
        for l in range(s // 128):
            lanes = slice(l * 128, (l + 1) * 128)
            v = [tab[pl.ds(h * LO + row, 8), lanes] for h in range(n_hi)]
            step = 1
            while step < n_hi:
                for a in range(n_hi):
                    if not a & step:
                        v[a], v[a + step] = v[a] + v[a + step], v[a] - v[a + step]
                step *= 2
            for h in range(n_hi):
                tab[pl.ds(h * LO + row, 8), lanes] = v[h]
                for j in range(1, n_top):
                    tab[pl.ds((j * n_hi + h) * LO + row, 8), lanes] = v[h] * sgn[j]
        return 0

    lax.fori_loop(0, LO // 8, column, 0)


def transform(frames, scale_rows, sgn):
    f, s = frames.shape
    n_hi, n_top = f // LO, sgn.shape[0]
    parts = 8
    return pl.pallas_call(
        functools.partial(transform_kernel, n_hi=n_hi, n_top=n_top, parts=parts),
        out_shape=jax.ShapeDtypeStruct((n_top * f, s), F32),
        in_specs=[SMEM, HBM, VMEM],
        out_specs=VMEM,
        scratch_shapes=[
            pltpu.VMEM((LO, LO), F32),
            pltpu.VMEM((f, s), BF16),
            pltpu.SemaphoreType.DMA((parts,)),
        ],
        cost_estimate=cost(f * s),
        compiler_params=params(24),
    )(sgn, pltpu.with_memory_space_constraint(frames, pltpu.HBM), scale_rows)


def gather_kernel(codes, tab, *refs, base, group, n_dep, n_out):
    for o_ref in refs[n_dep : n_dep + n_out]:

        def some(t, _, o_ref=o_ref, base=base):
            at = pl.multiple_of(t * group, group)
            rows = [tab[pl.ds(codes[base + at + m], 1), :] for m in range(group)]
            o_ref[pl.ds(at, group), :] = jnp.concatenate(rows, axis=0).astype(BF16)
            return 0

        lax.fori_loop(0, o_ref.shape[0] // group, some, 0)
        base += o_ref.shape[0]


def gather(table, codes, base, n, deps=(), passing=(), group=16):
    s = table.shape[1]
    return pl.pallas_call(
        functools.partial(
            gather_kernel, base=base, group=group, n_dep=len(deps) + len(passing), n_out=1
        ),
        out_shape=[jax.ShapeDtypeStruct((n, s), BF16)]
        + [jax.ShapeDtypeStruct(v.shape, v.dtype) for v in passing],
        in_specs=[SMEM, VMEM] + [ANY] * (len(passing) + len(deps)),
        out_specs=[VMEM] + [ANY] * len(passing),
        input_output_aliases={2 + i: 1 + i for i in range(len(passing))},
        cost_estimate=cost(n * s),
        compiler_params=params(20),
    )(codes, table, *passing, *deps)


def pick_kernel(act, own, sent, o_ref, *, reach):
    o_ref[...] = jnp.where(act[0] >= reach, sent[...], own[...])


def pick(own, sent, act_pos, reach):
    n = own.shape[0]
    return pl.pallas_call(
        functools.partial(pick_kernel, reach=reach),
        out_shape=jax.ShapeDtypeStruct((n // 128, 128), jnp.int32),
        in_specs=[SMEM, VMEM, VMEM],
        out_specs=VMEM,
        cost_estimate=cost(n),
        compiler_params=params(2),
    )(act_pos.reshape(1), own.reshape(n // 128, 128), sent.reshape(n // 128, 128)).reshape(n)


def combine_kernel(*refs, n, columns, split, scale, n_dep):
    outs = refs[n + sum(columns) + n_dep :]
    for k in range(split if n else 0):
        rows = slice(k * outs[k].shape[0], (k + 1) * outs[k].shape[0])
        total = refs[0][rows, :].astype(F32)
        for r in refs[1:n]:
            total = total + r[rows, :].astype(F32)
        outs[k][...] = (total * scale).astype(BF16)
    at = n
    for length, out in zip(columns, outs[split if n else 0 :]):
        for j in range(length):
            rows = refs[at].shape[0]
            out[j * rows : (j + 1) * rows, :] = refs[at][...]
            at += 1


def combine(parts, columns, scale, deps=(), split=1, passing=()):
    shapes = []
    if parts:
        n, s = parts[0].shape
        shapes += [jax.ShapeDtypeStruct((n // split, s), BF16)] * split
    for column in columns:
        shapes.append(jax.ShapeDtypeStruct((len(column) * column[0].shape[0], column[0].shape[1]), BF16))
    arrays = list(parts) + [v for column in columns for v in column]
    out = pl.pallas_call(
        functools.partial(
            combine_kernel,
            n=len(parts),
            columns=[len(column) for column in columns],
            split=split,
            scale=scale,
            n_dep=len(passing) + len(deps),
        ),
        out_shape=shapes + [jax.ShapeDtypeStruct(v.shape, v.dtype) for v in passing],
        in_specs=[VMEM] * len(arrays) + [ANY] * (len(passing) + len(deps)),
        out_specs=[VMEM] * len(shapes) + [ANY] * len(passing),
        input_output_aliases={len(arrays) + i: len(shapes) + i for i in range(len(passing))},
        cost_estimate=cost(shapes[0].size),
        compiler_params=params(12),
    )(*arrays, *passing, *deps)
    n = split if parts else 0
    return list(out[:n]), list(out[n : len(shapes)]), list(out[len(shapes) :])


def across(v, lane):
    return jnp.broadcast_to(v[:, lane : lane + 1], (8, 128))


def down(v, row):
    return jnp.broadcast_to(v[row : row + 1, :], (8, 128))


def factor_tile(tile):
    lanes = lax.broadcasted_iota(jnp.int32, (8, 128), 1)
    subs = lax.broadcasted_iota(jnp.int32, (8, 128), 0)
    n = B // 8
    m = [tile[8 * g : 8 * g + 8, :] for g in range(n)]
    d = [across(m[0], k) for k in range(8)]
    upper, inverse = [], []
    for q in range(n):
        o = 8 * q
        done = lanes < o + 8
        here = done & (lanes >= o)
        s = {(i, j): down(d[j], i) for j in range(8) for i in range(j, 8)}
        e = jnp.where(lanes < o, m[q], jnp.where(lanes == subs + o, 1.0, 0.0))
        r = [down(m[q], i) for i in range(8)]
        t = [down(e, i) for i in range(8)]
        near = range(q + 1, min(q + 1 + NEAR, n))
        far = range(q + 1 + NEAR, n)
        c = {g: [across(m[g], o + j) for j in range(8)] for g in range(q + 1, n)}
        if q + 1 < n:
            d = [across(m[q + 1], o + 8 + k) for k in range(8)]
        for g in range(q + 1, n):
            m[g] = jnp.where(here, 0.0, m[g])
        root, u, w, z = [], [], [], []
        for j in range(8):
            root.append(lax.rsqrt(s[j, j]))
            for i in range(j + 1, 8):
                s[i, j] = s[i, j] * root[j]
            for i in range(j + 1, 8):
                for k in range(j + 1, i + 1):
                    s[i, k] = s[i, k] - s[i, j] * s[k, j]
            u.append(r[j] * root[j])
            w.append(t[j] * root[j])
            z.append(jnp.where(done, w[j], u[j]))
            for i in range(j + 1, 8):
                r[i] = r[i] - s[i, j] * u[j]
                t[i] = t[i] - s[i, j] * w[j]
            for g in near:
                column = c[g][j] * root[j]
                for k in range(j + 1, 8):
                    c[g][k] = c[g][k] - column * s[k, j]
                m[g] = m[g] - column * z[j]
                if g == q + 1:
                    for k in range(8):
                        d[k] = d[k] - column * down(column, k)
        u_rows, w_rows = u[0], w[0]
        for j in range(1, 8):
            u_rows = jnp.where(subs == j, u[j], u_rows)
            w_rows = jnp.where(subs == j, w[j], w_rows)
        upper.append(jnp.where(lanes >= subs + o, u_rows, 0.0))
        inverse.append(w_rows)
        if far:
            for j in reversed(range(8)):
                for i in range(j + 1, 8):
                    z[j] = z[j] - s[i, j] * z[i]
                z[j] = z[j] * root[j]
            for g in far:
                for j in range(8):
                    m[g] = m[g] - c[g][j] * z[j]
    return upper, inverse


def join(pair, out, pos, start=0, n=None):
    n_slope = pos.shape[0] - 1
    s_dev = pair[0].shape[1]
    size = pair[0].shape[0] * 2 // n_slope
    for j in range(n_slope):
        source, at = pair[j * 2 // n_slope], j % (n_slope // 2) * size + start
        out[:, pl.ds(pl.multiple_of(pos[1 + j] * s_dev, s_dev), s_dev)] = source[at : at + (n or size), :]


def against(left, right):
    return lax.dot_general(left, right, (((1,), (1,)), ((), ())), preferred_element_type=F32)


def on_diagonal(assign, loads):
    n = assign.shape[1]
    load = jnp.zeros((1, n), F32)
    for m in range(NDM):
        load = jnp.where(assign == m, loads[m], load)
    r = lax.broadcasted_iota(jnp.int32, (n, n), 0)
    c = lax.broadcasted_iota(jnp.int32, (n, n), 1)
    return jnp.where(r == c, load, 0.0)


def factor_block(u_ref, inverse, k):
    o = pl.multiple_of(k * B, B)
    upper, inv = factor_tile(u_ref[pl.ds(o, B), pl.ds(o, B)])
    for g in range(B // 8):
        u_ref[pl.ds(o + 8 * g, 8), pl.ds(o, B)] = upper[g]
        inverse[8 * g : 8 * g + 8, :] = inv[g]


def eliminate(u_ref, inverse, k, start):
    top = slice(k * B, (k + 1) * B)
    strip = jnp.dot(inverse, u_ref[top, start:], precision=HIGHEST, preferred_element_type=F32)
    u_ref[top, start:] = strip
    return strip


def trailing(u_ref, k, rows, cols):
    top = slice(k * B, (k + 1) * B)
    u_ref[rows, cols] = u_ref[rows, cols] - lax.dot_general(
        u_ref[top, rows],
        u_ref[top, cols],
        (((0,), (0,)), ((), ())),
        precision=HIGHEST,
        preferred_element_type=F32,
    )


def bands(start, stop, height=256):
    return [
        (slice(r, min(r + height, stop)), slice(r, stop)) for r in range(start, stop, height)
    ]


def factor_loop(u_ref, inverse, first, last):
    n = u_ref.shape[0]

    def body(k, _):
        factor_block(u_ref, inverse.at[k - first], k)
        for kk in range(first, last):
            if (kk + 1) * B < n:

                @pl.when(k == kk)
                def _():
                    r0 = (kk + 1) * B
                    eliminate(u_ref, inverse[kk - first], kk, r0)
                    for rows, cols in bands(r0, n):
                        trailing(u_ref, kk, rows, cols)

        return 0

    lax.fori_loop(first, last, body, 0)


def head_kernel(pos, loads, assign, *refs, total_rows, n_dep):
    left, u_ref, inverse = refs[2 + n_dep :]
    join(refs[:2], left, pos)
    n = u_ref.shape[0]
    u_ref[...] = against(left[...], left[...]) * (1.0 / total_rows) + on_diagonal(assign[:, :n], loads)
    factor_loop(u_ref, inverse, 0, u_ref.shape[0] // B)


def factor_head(pieces, loads, assign, pos, total_rows, deps=()):
    n = pieces[0].shape[0] * pieces[0].shape[1] * 2 // total_rows
    return pl.pallas_call(
        functools.partial(head_kernel, total_rows=total_rows, n_dep=len(deps)),
        out_shape=[
            jax.ShapeDtypeStruct((n, total_rows), BF16),
            jax.ShapeDtypeStruct((n, n), F32),
            jax.ShapeDtypeStruct((n // B, B, B), F32),
        ],
        in_specs=[SMEM] * 2 + [VMEM] * 3 + [ANY] * len(deps),
        out_specs=[VMEM] * 3,
        cost_estimate=cost(1 << 20),
        compiler_params=params(18),
    )(pos, loads, assign, *pieces, *deps)


def middle_kernel(pos, loads, assign, *refs, total_rows, n_dep, last):
    left0, u0, inv0 = refs[2:5]
    right, u_ref, left1, inverse = refs[5 + n_dep :]
    join(refs[:2], left1, pos)
    h, n = u0.shape[0], u_ref.shape[0]
    right[:, :h] = left0[...].T
    right[:, h:] = left1[...].T
    u_ref[:h, :h] = u0[...]
    u_ref[:h, h:] = jnp.dot(left0[...], right[:, h:], preferred_element_type=F32) * (1.0 / total_rows)
    for rows, cols in bands(h, n):
        u_ref[rows, cols] = jnp.dot(
            left1[rows.start - h : rows.stop - h, :], right[:, cols], preferred_element_type=F32
        ) * (1.0 / total_rows)
        u_ref[rows, rows] = u_ref[rows, rows] + on_diagonal(assign[:, rows], loads)
    for k in range(h // B):
        eliminate(u_ref, inv0[k], k, h)
        if (k + 1) * B < h:
            trailing(u_ref, k, slice((k + 1) * B, h), slice(h, n))
    for rows, cols in bands(h, n):
        u_ref[rows, cols] = u_ref[rows, cols] - lax.dot_general(
            u_ref[:h, rows],
            u_ref[:h, cols],
            (((0,), (0,)), ((), ())),
            precision=HIGHEST,
            preferred_element_type=F32,
        )
    factor_loop(u_ref, inverse, h // B, last)


def factor_middle(pieces, loads, assign, head, pos, total_rows, last, deps=()):
    left0, u0, inv0 = head
    below = pieces[0].shape[0] * pieces[0].shape[1] * 2 // total_rows
    n = below + u0.shape[0]
    return pl.pallas_call(
        functools.partial(middle_kernel, total_rows=total_rows, n_dep=len(deps), last=last),
        out_shape=[jax.ShapeDtypeStruct((total_rows, n), BF16), jax.ShapeDtypeStruct((n, n), F32)],
        in_specs=[SMEM] * 2 + [VMEM] * 6 + [ANY] * len(deps),
        out_specs=[VMEM] * 2,
        scratch_shapes=[
            pltpu.VMEM((below, total_rows), BF16),
            pltpu.VMEM((last - u0.shape[0] // B, B, B), F32),
        ],
        cost_estimate=cost(1 << 20),
        compiler_params=params(18),
    )(pos, loads, assign, *pieces, left0, u0, inv0, *deps)


def tail_kernel(pos, u_in, *refs, first, last, n_dep):
    u_ref, token, inverse = refs[n_dep:]
    factor_loop(u_ref, inverse, first, last)
    token[...] = jnp.zeros_like(token)


def factor_more(u, pos, first, last, deps=()):
    return pl.pallas_call(
        functools.partial(tail_kernel, first=first, last=last, n_dep=len(deps)),
        out_shape=[jax.ShapeDtypeStruct(u.shape, F32), TOKEN],
        in_specs=[SMEM, VMEM] + [ANY] * len(deps),
        out_specs=[VMEM] * 2,
        scratch_shapes=[pltpu.VMEM((last - first, B, B), F32)],
        input_output_aliases={1: 0},
        cost_estimate=cost(1 << 20),
        compiler_params=params(18),
    )(pos, u, *deps)


def rows_kernel(pos, u_ref, *refs, block, n_dep):
    o_ref, token, rows = refs[n_dep:]
    token[...] = jnp.zeros_like(token)
    width = u_ref.shape[1]
    wide = rows.shape[0]
    first = pos[0] * block
    base = first // wide * wide
    rows[...] = u_ref[:, pl.ds(pl.multiple_of(base, wide), wide)].T
    own = rows[pl.ds(pl.multiple_of(first - base, 8), block), :]
    row_ids = first + lax.broadcasted_iota(jnp.int32, (block, width), 0)
    col_ids = lax.broadcasted_iota(jnp.int32, (block, width), 1)
    o_ref[...] = jnp.where(row_ids >= col_ids, own, 0.0)


def own_rows(u, pos, block, deps=()):
    width = u.shape[1]
    return pl.pallas_call(
        functools.partial(rows_kernel, block=block, n_dep=len(deps)),
        out_shape=[jax.ShapeDtypeStruct((block, width), F32), TOKEN],
        in_specs=[SMEM, VMEM] + [ANY] * len(deps),
        out_specs=[VMEM] * 2,
        scratch_shapes=[pltpu.VMEM((max(block, 128), width), F32)],
        cost_estimate=cost(block * width),
        compiler_params=params(10),
    )(pos, u, *deps)


def gram_kernel(pos, *refs, n, total_rows, n_dep, at, tile):
    right = refs[2]
    o_ref, token, left, buf, sems = refs[3 + n_dep :]
    token[...] = jnp.zeros_like(token)
    copies = []
    for t in range(n // tile):
        join(refs[:2], left, pos, t * tile, tile)
        if t >= 2:
            copies[t - 2].wait()
        buf[t % 2] = jnp.dot(left[...], right[...], preferred_element_type=F32) * (1.0 / total_rows)
        copies.append(
            pltpu.make_async_copy(buf.at[t % 2], o_ref.at[pl.ds(at + t * tile, tile), :], sems.at[t % 2])
        )
        copies[-1].start()
    for copy in copies[-2:]:
        copy.wait()


def gram_rows(pieces, right, pos, out, at, total, deps=(), tile=512):
    total_rows, width = right.shape
    n = pieces[0].shape[0] * pieces[0].shape[1] * 2 // total_rows
    deps = ((out,) if out is not None else ()) + tuple(deps)
    return pl.pallas_call(
        functools.partial(
            gram_kernel, n=n, total_rows=total_rows, n_dep=len(deps), at=at, tile=tile
        ),
        out_shape=[jax.ShapeDtypeStruct((total, width), F32), TOKEN],
        in_specs=[SMEM] + [VMEM] * 3 + [ANY] * len(deps),
        out_specs=[HBM, VMEM],
        scratch_shapes=[
            pltpu.VMEM((tile, total_rows), BF16),
            pltpu.VMEM((2, tile, width), F32),
            pltpu.SemaphoreType.DMA((2,)),
        ],
        input_output_aliases={} if out is None else {4: 0},
        cost_estimate=cost(n * width),
        compiler_params=params(12),
    )(pos, *pieces, right, *deps)


def local(frames, frame_scale, codes, assign, loads):
    f_dev, s_dev = frames.shape
    a_dev = codes.shape[0]
    n_tm, n_slope, n_act = lax.axis_size("tm"), lax.axis_size("slope"), lax.axis_size("act")
    tm_pos, slope_pos, act_pos = lax.axis_index("tm"), lax.axis_index("slope"), lax.axis_index("act")
    scale = 1.0 / math.sqrt(f_dev * n_tm)
    total_rows = s_dev * n_slope
    block = PW // n_act
    n_y = n_slope // 2
    head = 256

    own_codes = codes[:PW]
    panel_codes = own_codes
    reach = 1
    while reach < n_act:
        sent = lax.ppermute(
            panel_codes, "act", [(i, i + reach) for i in range(min(reach, n_act - reach))]
        )
        panel_codes = pick(panel_codes, sent, act_pos, reach)
        reach *= 2
    scale_rows = frame_scale.astype(BF16).astype(F32).reshape(f_dev // LO, LO)
    sgn = (1 - 2 * parity_bits(lax.iota(jnp.int32, n_tm) & tm_pos)).astype(F32)
    y_pos, core_pos = slope_pos // 2, slope_pos % 2
    origin = [(y_pos - r + n_y) % n_y for r in range(n_y)]
    pos = jnp.stack(
        [act_pos] + [2 * y + core_pos for y in origin] + [2 * y + 1 - core_pos for y in origin]
    ).astype(jnp.int32)
    assign = assign[None, :]

    def over_tm(part):
        return [part] + [
            lax.ppermute(part, "tm", [(i, (i + r) % n_tm) for i in range(n_tm)]) for r in range(1, n_tm)
        ]

    def over_y(im):
        return [im] + [
            lax.ppermute(
                im,
                "slope",
                [(2 * y + k, 2 * ((y + r) % n_y) + k) for y in range(n_y) for k in range(2)],
            )
            for r in range(1, n_y)
        ]

    def over_core(column):
        return lax.ppermute(column, "slope", [(i, i ^ 1) for i in range(n_slope)])

    class Chunk:
        def __init__(self, im):
            self.column = over_y(im)

    def slot(parts=(), split=1, release=(), deps=(), passing=()):
        ims, columns, passed = combine(
            parts, [chunk.column for chunk in release], scale, deps, split, passing
        )
        for chunk, column in zip(release, columns):
            chunk.pieces = [column, over_core(column)]
        return [Chunk(im) for im in ims], (ims + columns)[0], passed

    table = transform(frames, scale_rows, sgn)
    several = a_dev >= 4096
    unit = a_dev // 4 if several else a_dev
    (p0,) = gather(table, panel_codes, 0, head)
    (p1,) = gather(table, panel_codes, head, PW - head, deps=(p0,))
    (m0,) = gather(table, codes, 0, unit, deps=(p1,))
    (p0,), dep, (p1,) = slot(over_tm(p0), deps=(m0,), passing=(p1,))
    p1 = over_tm(p1)
    if several:
        m1, m0 = gather(table, codes, unit, 2 * unit, deps=(dep,), passing=(m0,))
        m0 = over_tm(m0)
        m2, m1 = gather(table, codes, 3 * unit, unit, passing=(m1,))
        m1 = over_tm(m1)
        (p1,), dep, _ = slot(p1, release=[p0], deps=(m2,))
    else:
        m0 = over_tm(m0)
        (p1,), dep, _ = slot(p1, release=[p0])
    first = factor_head(p0.pieces, loads, assign, pos, total_rows, deps=(dep,))
    if several:
        chunks, dep, (m2,) = slot(m0, release=[p1], deps=(first[2],), passing=(m2,))
        m2 = over_tm(m2)
    else:
        chunks, dep, _ = slot(m0, release=[p1], deps=(first[2],))
    h, n_blocks = head // B, PW // B
    right, u = factor_middle(p1.pieces, loads, assign, first, pos, total_rows, h + 1, deps=(dep,))
    token = right
    out = None

    def more(k, dep):
        return factor_more(u, pos, k, k + 1, deps=(dep,))

    def gram(c, out, *deps):
        return gram_rows(chunks[c].pieces, right, pos, out, c * unit, a_dev, deps=deps)

    u, token = more(h + 1, token)
    if several:
        new, token, _ = slot(m1, 2, release=chunks[:1], deps=(token,))
        chunks += new
    else:
        _, token, _ = slot(release=chunks, deps=(token,))
    u, token = more(h + 2, token)
    u, token = more(h + 3, token)
    if several:
        new, token, _ = slot(m2, release=chunks[1:2], deps=(token,))
        chunks += new
    for c in range(2 if several else 0):
        out, token = gram(c, out, token, chunks[1].pieces[1])
    for k in range(h + 4, n_blocks - 1):
        u, token = more(k, token)
    if several:
        _, token, _ = slot(release=chunks[2:3], deps=(token,))
    u, token = more(n_blocks - 1, token)
    factor, token = own_rows(u, pos, block, deps=(token,))
    if several:
        _, token, _ = slot(release=chunks[3:], deps=(token,))
        out, token = gram(2, out, token)
    out, token = gram(len(chunks) - 1, out, token)
    return (out, factor)


def solution(mesh):
    return jax.shard_map(
        local,
        mesh=mesh,
        in_specs=(P("tm", "slope"), P("tm"), P("act"), P(), P()),
        out_specs=(P("act", None), P("act", None)),
        check_vma=False,
    )
```

```python
import functools
import math

import jax
import jax.numpy as jnp
from jax import lax
from jax.experimental import pallas as pl
from jax.experimental.pallas import tpu as pltpu
from jax.sharding import PartitionSpec as P

PW = 1024
NDM = 3
F32 = jnp.float32
BF16 = jnp.bfloat16
TOKEN = jax.ShapeDtypeStruct((8, 128), F32)
LO = 256
B = 128
NEAR = 3
HIGHEST = lax.Precision.HIGHEST


def parity_bits(values):
    for shift_by in (16, 8, 4, 2, 1):
        values = jnp.bitwise_xor(values, jnp.right_shift(values, shift_by))
    return jnp.bitwise_and(values, 1)


ANY = pl.BlockSpec(memory_space=pl.ANY)
VMEM = pl.BlockSpec(memory_space=pltpu.VMEM)
SMEM = pl.BlockSpec(memory_space=pltpu.SMEM)
HBM = pl.BlockSpec(memory_space=pltpu.HBM)


def params(mib):
    return pltpu.CompilerParams(vmem_limit_bytes=mib << 20)


def cost(elements):
    return pl.CostEstimate(flops=0, bytes_accessed=elements, transcendentals=0)


def transform_kernel(sgn, x_ref, w_ref, tab, had, buf, sems, *, n_hi, n_top, parts):
    s = x_ref.shape[1]
    per = n_hi // parts
    copies = [
        pltpu.make_async_copy(
            x_ref.at[pl.ds(p * per * LO, per * LO), :], buf.at[pl.ds(p * per * LO, per * LO), :], sems.at[p]
        )
        for p in range(parts)
    ]
    for copy in copies:
        copy.start()
    r = lax.broadcasted_iota(jnp.int32, (LO, LO), 0)
    c = lax.broadcasted_iota(jnp.int32, (LO, LO), 1)
    had[...] = (1 - 2 * parity_bits(r & c)).astype(F32)
    for p in range(parts):
        copies[p].wait()
        for k in range(p * per, (p + 1) * per):
            weights = (had[...] * w_ref[k : k + 1, :]).astype(BF16)
            tab[k * LO : (k + 1) * LO, :] = jnp.dot(
                weights, buf[k * LO : (k + 1) * LO, :], preferred_element_type=F32
            )

    def column(t, _):
        row = pl.multiple_of(t * 8, 8)
        for l in range(s // 128):
            lanes = slice(l * 128, (l + 1) * 128)
            v = [tab[pl.ds(h * LO + row, 8), lanes] for h in range(n_hi)]
            step = 1
            while step < n_hi:
                for a in range(n_hi):
                    if not a & step:
                        v[a], v[a + step] = v[a] + v[a + step], v[a] - v[a + step]
                step *= 2
            for h in range(n_hi):
                tab[pl.ds(h * LO + row, 8), lanes] = v[h]
                for j in range(1, n_top):
                    tab[pl.ds((j * n_hi + h) * LO + row, 8), lanes] = v[h] * sgn[j]
        return 0

    lax.fori_loop(0, LO // 8, column, 0)


def transform(frames, scale_rows, sgn):
    f, s = frames.shape
    n_hi, n_top = f // LO, sgn.shape[0]
    parts = 8
    return pl.pallas_call(
        functools.partial(transform_kernel, n_hi=n_hi, n_top=n_top, parts=parts),
        out_shape=jax.ShapeDtypeStruct((n_top * f, s), F32),
        in_specs=[SMEM, HBM, VMEM],
        out_specs=VMEM,
        scratch_shapes=[
            pltpu.VMEM((LO, LO), F32),
            pltpu.VMEM((f, s), BF16),
            pltpu.SemaphoreType.DMA((parts,)),
        ],
        cost_estimate=cost(f * s),
        compiler_params=params(24),
    )(sgn, pltpu.with_memory_space_constraint(frames, pltpu.HBM), scale_rows)


def gather_kernel(codes, tab, *refs, base, group, n_dep, n_out):
    for o_ref in refs[n_dep : n_dep + n_out]:

        def some(t, _, o_ref=o_ref, base=base):
            at = pl.multiple_of(t * group, group)
            rows = [tab[pl.ds(codes[base + at + m], 1), :] for m in range(group)]
            o_ref[pl.ds(at, group), :] = jnp.concatenate(rows, axis=0).astype(BF16)
            return 0

        lax.fori_loop(0, o_ref.shape[0] // group, some, 0)
        base += o_ref.shape[0]


def gather(table, codes, base, n, deps=(), passing=(), group=64):
    s = table.shape[1]
    return pl.pallas_call(
        functools.partial(
            gather_kernel, base=base, group=group, n_dep=len(deps) + len(passing), n_out=1
        ),
        out_shape=[jax.ShapeDtypeStruct((n, s), BF16)]
        + [jax.ShapeDtypeStruct(v.shape, v.dtype) for v in passing],
        in_specs=[SMEM, VMEM] + [ANY] * (len(passing) + len(deps)),
        out_specs=[VMEM] + [ANY] * len(passing),
        input_output_aliases={2 + i: 1 + i for i in range(len(passing))},
        cost_estimate=cost(n * s),
        compiler_params=params(20),
    )(codes, table, *passing, *deps)


def pick_kernel(act, own, sent, o_ref, *, reach):
    o_ref[...] = jnp.where(act[0] >= reach, sent[...], own[...])


def pick(own, sent, act_pos, reach):
    n = own.shape[0]
    return pl.pallas_call(
        functools.partial(pick_kernel, reach=reach),
        out_shape=jax.ShapeDtypeStruct((n // 128, 128), jnp.int32),
        in_specs=[SMEM, VMEM, VMEM],
        out_specs=VMEM,
        cost_estimate=cost(n),
        compiler_params=params(2),
    )(act_pos.reshape(1), own.reshape(n // 128, 128), sent.reshape(n // 128, 128)).reshape(n)


def combine_kernel(*refs, n, columns, split, scale, n_dep):
    outs = refs[n + sum(columns) + n_dep :]
    for k in range(split if n else 0):
        rows = slice(k * outs[k].shape[0], (k + 1) * outs[k].shape[0])
        total = refs[0][rows, :].astype(F32)
        for r in refs[1:n]:
            total = total + r[rows, :].astype(F32)
        outs[k][...] = (total * scale).astype(BF16)
    at = n
    for length, out in zip(columns, outs[split if n else 0 :]):
        for j in range(length):
            rows = refs[at].shape[0]
            out[j * rows : (j + 1) * rows, :] = refs[at][...]
            at += 1


def combine(parts, columns, scale, deps=(), split=1, passing=()):
    shapes = []
    if parts:
        n, s = parts[0].shape
        shapes += [jax.ShapeDtypeStruct((n // split, s), BF16)] * split
    for column in columns:
        shapes.append(jax.ShapeDtypeStruct((len(column) * column[0].shape[0], column[0].shape[1]), BF16))
    arrays = list(parts) + [v for column in columns for v in column]
    out = pl.pallas_call(
        functools.partial(
            combine_kernel,
            n=len(parts),
            columns=[len(column) for column in columns],
            split=split,
            scale=scale,
            n_dep=len(passing) + len(deps),
        ),
        out_shape=shapes + [jax.ShapeDtypeStruct(v.shape, v.dtype) for v in passing],
        in_specs=[VMEM] * len(arrays) + [ANY] * (len(passing) + len(deps)),
        out_specs=[VMEM] * len(shapes) + [ANY] * len(passing),
        input_output_aliases={len(arrays) + i: len(shapes) + i for i in range(len(passing))},
        cost_estimate=cost(shapes[0].size),
        compiler_params=params(12),
    )(*arrays, *passing, *deps)
    n = split if parts else 0
    return list(out[:n]), list(out[n : len(shapes)]), list(out[len(shapes) :])


def across(v, lane):
    return jnp.broadcast_to(v[:, lane : lane + 1], (8, 128))


def down(v, row):
    return jnp.broadcast_to(v[row : row + 1, :], (8, 128))


def factor_tile(tile):
    lanes = lax.broadcasted_iota(jnp.int32, (8, 128), 1)
    subs = lax.broadcasted_iota(jnp.int32, (8, 128), 0)
    n = B // 8
    m = [tile[8 * g : 8 * g + 8, :] for g in range(n)]
    d = [across(m[0], k) for k in range(8)]
    upper, inverse = [], []
    for q in range(n):
        o = 8 * q
        done = lanes < o + 8
        here = done & (lanes >= o)
        s = {(i, j): down(d[j], i) for j in range(8) for i in range(j, 8)}
        e = jnp.where(lanes < o, m[q], jnp.where(lanes == subs + o, 1.0, 0.0))
        r = [down(m[q], i) for i in range(8)]
        t = [down(e, i) for i in range(8)]
        near = range(q + 1, min(q + 1 + NEAR, n))
        far = range(q + 1 + NEAR, n)
        c = {g: [across(m[g], o + j) for j in range(8)] for g in range(q + 1, n)}
        if q + 1 < n:
            d = [across(m[q + 1], o + 8 + k) for k in range(8)]
        for g in range(q + 1, n):
            m[g] = jnp.where(here, 0.0, m[g])
        root, u, w, z = [], [], [], []
        for j in range(8):
            root.append(lax.rsqrt(s[j, j]))
            for i in range(j + 1, 8):
                s[i, j] = s[i, j] * root[j]
            for i in range(j + 1, 8):
                for k in range(j + 1, i + 1):
                    s[i, k] = s[i, k] - s[i, j] * s[k, j]
            u.append(r[j] * root[j])
            w.append(t[j] * root[j])
            z.append(jnp.where(done, w[j], u[j]))
            for i in range(j + 1, 8):
                r[i] = r[i] - s[i, j] * u[j]
                t[i] = t[i] - s[i, j] * w[j]
            for g in near:
                column = c[g][j] * root[j]
                for k in range(j + 1, 8):
                    c[g][k] = c[g][k] - column * s[k, j]
                m[g] = m[g] - column * z[j]
                if g == q + 1:
                    for k in range(8):
                        d[k] = d[k] - column * down(column, k)
        u_rows, w_rows = u[0], w[0]
        for j in range(1, 8):
            u_rows = jnp.where(subs == j, u[j], u_rows)
            w_rows = jnp.where(subs == j, w[j], w_rows)
        upper.append(jnp.where(lanes >= subs + o, u_rows, 0.0))
        inverse.append(w_rows)
        if far:
            for j in reversed(range(8)):
                for i in range(j + 1, 8):
                    z[j] = z[j] - s[i, j] * z[i]
                z[j] = z[j] * root[j]
            for g in far:
                for j in range(8):
                    m[g] = m[g] - c[g][j] * z[j]
    return upper, inverse


def join(pair, out, pos, start=0, n=None):
    n_slope = pos.shape[0] - 1
    s_dev = pair[0].shape[1]
    size = pair[0].shape[0] * 2 // n_slope
    for j in range(n_slope):
        source, at = pair[j * 2 // n_slope], j % (n_slope // 2) * size + start
        out[:, pl.ds(pl.multiple_of(pos[1 + j] * s_dev, s_dev), s_dev)] = source[at : at + (n or size), :]


def against(left, right):
    return lax.dot_general(left, right, (((1,), (1,)), ((), ())), preferred_element_type=F32)


def on_diagonal(assign, loads):
    n = assign.shape[1]
    load = jnp.zeros((1, n), F32)
    for m in range(NDM):
        load = jnp.where(assign == m, loads[m], load)
    r = lax.broadcasted_iota(jnp.int32, (n, n), 0)
    c = lax.broadcasted_iota(jnp.int32, (n, n), 1)
    return jnp.where(r == c, load, 0.0)


def factor_block(u_ref, inverse, k):
    o = pl.multiple_of(k * B, B)
    upper, inv = factor_tile(u_ref[pl.ds(o, B), pl.ds(o, B)])
    for g in range(B // 8):
        u_ref[pl.ds(o + 8 * g, 8), pl.ds(o, B)] = upper[g]
        inverse[8 * g : 8 * g + 8, :] = inv[g]


def eliminate(u_ref, inverse, k, start):
    top = slice(k * B, (k + 1) * B)
    strip = jnp.dot(inverse, u_ref[top, start:], precision=HIGHEST, preferred_element_type=F32)
    u_ref[top, start:] = strip
    return strip


def trailing(u_ref, k, rows, cols):
    top = slice(k * B, (k + 1) * B)
    u_ref[rows, cols] = u_ref[rows, cols] - lax.dot_general(
        u_ref[top, rows],
        u_ref[top, cols],
        (((0,), (0,)), ((), ())),
        precision=HIGHEST,
        preferred_element_type=F32,
    )


def bands(start, stop, height=256):
    return [
        (slice(r, min(r + height, stop)), slice(r, stop)) for r in range(start, stop, height)
    ]


def factor_loop(u_ref, inverse, first, last):
    n = u_ref.shape[0]

    def body(k, _):
        factor_block(u_ref, inverse.at[k - first], k)
        for kk in range(first, last):
            if (kk + 1) * B < n:

                @pl.when(k == kk)
                def _():
                    r0 = (kk + 1) * B
                    eliminate(u_ref, inverse[kk - first], kk, r0)
                    for rows, cols in bands(r0, n):
                        trailing(u_ref, kk, rows, cols)

        return 0

    lax.fori_loop(first, last, body, 0)


def head_kernel(pos, loads, assign, *refs, total_rows, n_dep):
    left, u_ref, inverse = refs[2 + n_dep :]
    join(refs[:2], left, pos)
    n = u_ref.shape[0]
    u_ref[...] = against(left[...], left[...]) * (1.0 / total_rows) + on_diagonal(assign[:, :n], loads)
    factor_loop(u_ref, inverse, 0, u_ref.shape[0] // B)


def factor_head(pieces, loads, assign, pos, total_rows, deps=()):
    n = pieces[0].shape[0] * pieces[0].shape[1] * 2 // total_rows
    return pl.pallas_call(
        functools.partial(head_kernel, total_rows=total_rows, n_dep=len(deps)),
        out_shape=[
            jax.ShapeDtypeStruct((n, total_rows), BF16),
            jax.ShapeDtypeStruct((n, n), F32),
            jax.ShapeDtypeStruct((n // B, B, B), F32),
        ],
        in_specs=[SMEM] * 2 + [VMEM] * 3 + [ANY] * len(deps),
        out_specs=[VMEM] * 3,
        cost_estimate=cost(1 << 20),
        compiler_params=params(18),
    )(pos, loads, assign, *pieces, *deps)


def middle_kernel(pos, loads, assign, *refs, total_rows, n_dep, last):
    left0, u0, inv0 = refs[2:5]
    right, u_ref, left1, inverse = refs[5 + n_dep :]
    join(refs[:2], left1, pos)
    h, n = u0.shape[0], u_ref.shape[0]
    right[:, :h] = left0[...].T
    right[:, h:] = left1[...].T
    u_ref[:h, :h] = u0[...]
    u_ref[:h, h:] = jnp.dot(left0[...], right[:, h:], preferred_element_type=F32) * (1.0 / total_rows)
    for rows, cols in bands(h, n):
        u_ref[rows, cols] = jnp.dot(
            left1[rows.start - h : rows.stop - h, :], right[:, cols], preferred_element_type=F32
        ) * (1.0 / total_rows)
        u_ref[rows, rows] = u_ref[rows, rows] + on_diagonal(assign[:, rows], loads)
    for k in range(h // B):
        eliminate(u_ref, inv0[k], k, h)
        if (k + 1) * B < h:
            trailing(u_ref, k, slice((k + 1) * B, h), slice(h, n))
    for rows, cols in bands(h, n):
        u_ref[rows, cols] = u_ref[rows, cols] - lax.dot_general(
            u_ref[:h, rows],
            u_ref[:h, cols],
            (((0,), (0,)), ((), ())),
            precision=HIGHEST,
            preferred_element_type=F32,
        )
    factor_loop(u_ref, inverse, h // B, last)


def factor_middle(pieces, loads, assign, head, pos, total_rows, last, deps=()):
    left0, u0, inv0 = head
    below = pieces[0].shape[0] * pieces[0].shape[1] * 2 // total_rows
    n = below + u0.shape[0]
    return pl.pallas_call(
        functools.partial(middle_kernel, total_rows=total_rows, n_dep=len(deps), last=last),
        out_shape=[jax.ShapeDtypeStruct((total_rows, n), BF16), jax.ShapeDtypeStruct((n, n), F32)],
        in_specs=[SMEM] * 2 + [VMEM] * 6 + [ANY] * len(deps),
        out_specs=[VMEM] * 2,
        scratch_shapes=[
            pltpu.VMEM((below, total_rows), BF16),
            pltpu.VMEM((last - u0.shape[0] // B, B, B), F32),
        ],
        cost_estimate=cost(1 << 20),
        compiler_params=params(18),
    )(pos, loads, assign, *pieces, left0, u0, inv0, *deps)


def tail_kernel(pos, u_in, *refs, first, last, n_dep):
    u_ref, token, inverse = refs[n_dep:]
    factor_loop(u_ref, inverse, first, last)
    token[...] = jnp.zeros_like(token)


def factor_more(u, pos, first, last, deps=()):
    return pl.pallas_call(
        functools.partial(tail_kernel, first=first, last=last, n_dep=len(deps)),
        out_shape=[jax.ShapeDtypeStruct(u.shape, F32), TOKEN],
        in_specs=[SMEM, VMEM] + [ANY] * len(deps),
        out_specs=[VMEM] * 2,
        scratch_shapes=[pltpu.VMEM((last - first, B, B), F32)],
        input_output_aliases={1: 0},
        cost_estimate=cost(1 << 20),
        compiler_params=params(18),
    )(pos, u, *deps)


def rows_kernel(pos, u_ref, *refs, block, n_dep):
    o_ref, token, rows = refs[n_dep:]
    token[...] = jnp.zeros_like(token)
    width = u_ref.shape[1]
    wide = rows.shape[0]
    first = pos[0] * block
    base = first // wide * wide
    rows[...] = u_ref[:, pl.ds(pl.multiple_of(base, wide), wide)].T
    own = rows[pl.ds(pl.multiple_of(first - base, 8), block), :]
    row_ids = first + lax.broadcasted_iota(jnp.int32, (block, width), 0)
    col_ids = lax.broadcasted_iota(jnp.int32, (block, width), 1)
    o_ref[...] = jnp.where(row_ids >= col_ids, own, 0.0)


def own_rows(u, pos, block, deps=()):
    width = u.shape[1]
    return pl.pallas_call(
        functools.partial(rows_kernel, block=block, n_dep=len(deps)),
        out_shape=[jax.ShapeDtypeStruct((block, width), F32), TOKEN],
        in_specs=[SMEM, VMEM] + [ANY] * len(deps),
        out_specs=[VMEM] * 2,
        scratch_shapes=[pltpu.VMEM((max(block, 128), width), F32)],
        cost_estimate=cost(block * width),
        compiler_params=params(10),
    )(pos, u, *deps)


def gram_kernel(pos, *refs, n, total_rows, n_dep, at, tile):
    right = refs[2]
    o_ref, token, left, buf, sems = refs[3 + n_dep :]
    token[...] = jnp.zeros_like(token)
    copies = []
    for t in range(n // tile):
        join(refs[:2], left, pos, t * tile, tile)
        if t >= 2:
            copies[t - 2].wait()
        buf[t % 2] = jnp.dot(left[...], right[...], preferred_element_type=F32) * (1.0 / total_rows)
        copies.append(
            pltpu.make_async_copy(buf.at[t % 2], o_ref.at[pl.ds(at + t * tile, tile), :], sems.at[t % 2])
        )
        copies[-1].start()
    for copy in copies[-2:]:
        copy.wait()


def gram_rows(pieces, right, pos, out, at, total, deps=(), tile=512):
    total_rows, width = right.shape
    n = pieces[0].shape[0] * pieces[0].shape[1] * 2 // total_rows
    deps = ((out,) if out is not None else ()) + tuple(deps)
    return pl.pallas_call(
        functools.partial(
            gram_kernel, n=n, total_rows=total_rows, n_dep=len(deps), at=at, tile=tile
        ),
        out_shape=[jax.ShapeDtypeStruct((total, width), F32), TOKEN],
        in_specs=[SMEM] + [VMEM] * 3 + [ANY] * len(deps),
        out_specs=[HBM, VMEM],
        scratch_shapes=[
            pltpu.VMEM((tile, total_rows), BF16),
            pltpu.VMEM((2, tile, width), F32),
            pltpu.SemaphoreType.DMA((2,)),
        ],
        input_output_aliases={} if out is None else {4: 0},
        cost_estimate=cost(n * width),
        compiler_params=params(12),
    )(pos, *pieces, right, *deps)


def local(frames, frame_scale, codes, assign, loads):
    f_dev, s_dev = frames.shape
    a_dev = codes.shape[0]
    n_tm, n_slope, n_act = lax.axis_size("tm"), lax.axis_size("slope"), lax.axis_size("act")
    tm_pos, slope_pos, act_pos = lax.axis_index("tm"), lax.axis_index("slope"), lax.axis_index("act")
    scale = 1.0 / math.sqrt(f_dev * n_tm)
    total_rows = s_dev * n_slope
    block = PW // n_act
    n_y = n_slope // 2
    head = 256

    own_codes = codes[:PW]
    panel_codes = own_codes
    reach = 1
    while reach < n_act:
        sent = lax.ppermute(
            panel_codes, "act", [(i, i + reach) for i in range(min(reach, n_act - reach))]
        )
        panel_codes = pick(panel_codes, sent, act_pos, reach)
        reach *= 2
    scale_rows = frame_scale.astype(BF16).astype(F32).reshape(f_dev // LO, LO)
    sgn = (1 - 2 * parity_bits(lax.iota(jnp.int32, n_tm) & tm_pos)).astype(F32)
    y_pos, core_pos = slope_pos // 2, slope_pos % 2
    origin = [(y_pos - r + n_y) % n_y for r in range(n_y)]
    pos = jnp.stack(
        [act_pos] + [2 * y + core_pos for y in origin] + [2 * y + 1 - core_pos for y in origin]
    ).astype(jnp.int32)
    assign = assign[None, :]

    def over_tm(part):
        return [part] + [
            lax.ppermute(part, "tm", [(i, (i + r) % n_tm) for i in range(n_tm)]) for r in range(1, n_tm)
        ]

    def over_y(im):
        return [im] + [
            lax.ppermute(
                im,
                "slope",
                [(2 * y + k, 2 * ((y + r) % n_y) + k) for y in range(n_y) for k in range(2)],
            )
            for r in range(1, n_y)
        ]

    def over_core(column):
        return lax.ppermute(column, "slope", [(i, i ^ 1) for i in range(n_slope)])

    class Chunk:
        def __init__(self, im):
            self.column = over_y(im)

    def slot(parts=(), split=1, release=(), deps=(), passing=()):
        ims, columns, passed = combine(
            parts, [chunk.column for chunk in release], scale, deps, split, passing
        )
        for chunk, column in zip(release, columns):
            chunk.pieces = [column, over_core(column)]
        return [Chunk(im) for im in ims], (ims + columns)[0], passed

    table = transform(frames, scale_rows, sgn)
    several = a_dev >= 4096
    unit = a_dev // 4 if several else a_dev
    (p0,) = gather(table, panel_codes, 0, head)
    (p1,) = gather(table, panel_codes, head, PW - head, deps=(p0,))
    (m0,) = gather(table, codes, 0, unit, deps=(p1,))
    (p0,), dep, (p1,) = slot(over_tm(p0), deps=(m0,), passing=(p1,))
    p1 = over_tm(p1)
    if several:
        m1, m0 = gather(table, codes, unit, 2 * unit, deps=(dep,), passing=(m0,))
        m0 = over_tm(m0)
        m2, m1 = gather(table, codes, 3 * unit, unit, passing=(m1,))
        m1 = over_tm(m1)
        (p1,), dep, _ = slot(p1, release=[p0], deps=(m2,))
    else:
        m0 = over_tm(m0)
        (p1,), dep, _ = slot(p1, release=[p0])
    first = factor_head(p0.pieces, loads, assign, pos, total_rows, deps=(dep,))
    if several:
        chunks, dep, (m2,) = slot(m0, release=[p1], deps=(first[2],), passing=(m2,))
        m2 = over_tm(m2)
    else:
        chunks, dep, _ = slot(m0, release=[p1], deps=(first[2],))
    h, n_blocks = head // B, PW // B
    right, u = factor_middle(p1.pieces, loads, assign, first, pos, total_rows, h + 1, deps=(dep,))
    token = right
    out = None

    def more(k, dep):
        return factor_more(u, pos, k, k + 1, deps=(dep,))

    def gram(c, out, *deps):
        return gram_rows(chunks[c].pieces, right, pos, out, c * unit, a_dev, deps=deps)

    u, token = more(h + 1, token)
    if several:
        new, token, _ = slot(m1, 2, release=chunks[:1], deps=(token,))
        chunks += new
    else:
        _, token, _ = slot(release=chunks, deps=(token,))
    u, token = more(h + 2, token)
    u, token = more(h + 3, token)
    if several:
        new, token, _ = slot(m2, release=chunks[1:2], deps=(token,))
        chunks += new
    for c in range(2 if several else 0):
        out, token = gram(c, out, token, chunks[1].pieces[1])
    for k in range(h + 4, n_blocks - 1):
        u, token = more(k, token)
    if several:
        _, token, _ = slot(release=chunks[2:3], deps=(token,))
    u, token = more(n_blocks - 1, token)
    factor, token = own_rows(u, pos, block, deps=(token,))
    if several:
        _, token, _ = slot(release=chunks[3:], deps=(token,))
        out, token = gram(2, out, token)
    out, token = gram(len(chunks) - 1, out, token)
    return (out, factor)


def solution(mesh):
    return jax.shard_map(
        local,
        mesh=mesh,
        in_specs=(P("tm", "slope"), P("tm"), P("act"), P(), P()),
        out_specs=(P("act", None), P("act", None)),
        check_vma=False,
    )
```
